256 devices in a mesh: gx: 8 (over x, core), gy: 32 (over y, z).
Axes of the slice: x: 4, y: 4, z: 8, core: 2. Of those that a mesh axis runs over, the one named last changes fastest.
Arguments:
- forcing: float32 [8, 8, 8, 8, 32, 128], P(None, None, None, 'gx', 'gy'), may hold values from -6 to 6
- coefficient: float32 [8, 8, 8, 8, 32, 128], P(None, None, None, 'gx', 'gy'), may hold values from 0.3 to 3
Outputs:
- pressure: float32 [8, 8, 8, 8, 32, 128], P(None, None, None, 'gx', 'gy')
- residual: float32 [8, 8, 8, 8, 32, 128], P(None, None, None, 'gx', 'gy')
The draws below stay inside these ranges and needn't reach their ends.
All inputs are finite; a program needn't handle non-finite values.
Results may differ from the reference program's by a relative error of at most 0.0003.
Values sent between devices are 32-bit elements; how exact they have to be, the bound alone decides.
No kernel may reach another device: no remote copies, remote signals or barrier semaphores. Data moves between devices by JAX's collectives and lax.ppermute only.
A program may use at most 64 MiB of HBM per device.

```python
import math
import jax
import jax.numpy as jnp
from jax import lax

NP = 8
EZ = 128
ITERS = 2
EX = 8
EY = 32


def draw_forcing(key, part):
    node_key = jax.random.fold_in(key, 11)
    elem_key = jax.random.fold_in(key, 12)
    full_shape = (NP, NP, NP, EX, EY, EZ)
    nodal = jax.random.normal(node_key, full_shape, jnp.float32)
    element_part = 0.5 * jax.random.normal(elem_key, (EX, EY, EZ), jnp.float32)
    field = nodal + element_part[None, None, None]
    return jnp.clip(field, -6.0, 6.0).astype(jnp.float32)


def shard_levels(rng, dims, cuts, smallest, top_value):
    loudness = 1.0
    for dim, blocks in cuts:
        steps = jax.random.uniform(jax.random.fold_in(jax.random.fold_in(rng, 6), dim), (blocks,), jnp.float32, smallest / len(cuts), top_value / len(cuts))
        loudness = loudness * jnp.repeat(jnp.exp(steps), dims[dim] // blocks).reshape((-1,) + (1,) * (len(dims) - 1 - dim))
    return loudness


def setup_inputs(seed: int = 0) -> dict:
    seeds = jax.random.split(jax.random.key(seed), 3)
    forcing = draw_forcing(jax.random.fold_in(seeds[2], 71), 0)
    coefficient = jnp.clip(jnp.exp(math.log(3.0) - 2.3025851 * jax.random.uniform(seeds[1], (NP, NP, NP, EX, EY, EZ), jnp.float32) ** shard_levels(seeds[1], (NP, NP, NP, EX, EY, EZ), ((3, 8), (4, 32)), -0.2, 0.2)), 0.3, 3.0)
    return dict(forcing=forcing, coefficient=coefficient)


stretch = (1.0, 64.0, 1.0)

def legendre_value(order, position):
    prev_value = 1.0
    this_value = position
    for degree_now in range(2, order + 1):
        next_value = ((2 * degree_now - 1) * position * this_value - (degree_now - 1) * prev_value) / degree_now
        prev_value = this_value
        this_value = next_value
    return this_value

def gll_points():
    points = [-1.0]
    for node_index in range(1, 7):
        position = -math.cos(math.pi * node_index / 7.0)
        for newton_step in range(60):
            target = legendre_value(8, position) - legendre_value(6, position)
            slope = 15.0 * legendre_value(7, position)
            position = position - target / slope
        points.append(position)
    points.append(1.0)
    return points

def jacobi_eigen(matrix_in):
    order_n = len(matrix_in)
    work_mat = [list(one_row) for one_row in matrix_in]
    vectors = [[1.0 if row_index == col_index else 0.0 for col_index in range(order_n)] for row_index in range(order_n)]
    for sweep_index in range(40):
        for first_idx in range(order_n):
            for second_idx in range(first_idx + 1, order_n):
                rotation = 0.5 * math.atan2(2.0 * work_mat[first_idx][second_idx], work_mat[second_idx][second_idx] - work_mat[first_idx][first_idx])
                cosine = math.cos(rotation)
                sine_part = math.sin(rotation)
                for other in range(order_n):
                    left_val = work_mat[other][first_idx]
                    right_val = work_mat[other][second_idx]
                    work_mat[other][first_idx] = cosine * left_val - sine_part * right_val
                    work_mat[other][second_idx] = sine_part * left_val + cosine * right_val
                for other in range(order_n):
                    left_val = work_mat[first_idx][other]
                    right_val = work_mat[second_idx][other]
                    work_mat[first_idx][other] = cosine * left_val - sine_part * right_val
                    work_mat[second_idx][other] = sine_part * left_val + cosine * right_val
                for other in range(order_n):
                    left_val = vectors[other][first_idx]
                    right_val = vectors[other][second_idx]
                    vectors[other][first_idx] = cosine * left_val - sine_part * right_val
                    vectors[other][second_idx] = sine_part * left_val + cosine * right_val
    return ([work_mat[diag_index][diag_index] for diag_index in range(order_n)], vectors)

def spectral_tables():
    nodes = gll_points()
    values_at = [legendre_value(7, position) for position in nodes]
    weights = [2.0 / (56.0 * value_now * value_now) for value_now in values_at]
    derivative = [[0.0] * 8 for row_index in range(8)]
    for row_index in range(8):
        for col_index in range(8):
            if row_index != col_index:
                derivative[row_index][col_index] = values_at[row_index] / (values_at[col_index] * (nodes[row_index] - nodes[col_index]))
    derivative[0][0] = -14.0
    derivative[7][7] = 14.0
    stiffness = [[sum((derivative[mid][row_index] * weights[mid] * derivative[mid][col_index] for mid in range(8))) for col_index in range(8)] for row_index in range(8)]
    stiffness[0][0] = 2.0 * stiffness[0][0]
    stiffness[7][7] = 2.0 * stiffness[7][7]
    inv_root = [1.0 / math.sqrt(weight_now) for weight_now in weights]
    symmetric = [[inv_root[row_index] * stiffness[row_index][col_index] * inv_root[col_index] for col_index in range(8)] for row_index in range(8)]
    eigen_values, eigen_vectors = jacobi_eigen(symmetric)
    fdm_basis = [[inv_root[row_index] * eigen_vectors[row_index][col_index] for col_index in range(8)] for row_index in range(8)]
    linear_hat = [[(1.0 - position) / 2.0 for position in nodes], [(1.0 + position) / 2.0 for position in nodes]]
    return tuple((jnp.asarray(one_table, dtype=jnp.float32) for one_table in (weights, derivative, fdm_basis, eigen_values, linear_hat)))

def contract(form, table, field):
    return jnp.einsum(form, table, field, precision=lax.Precision.HIGHEST)

def edge_factors(local_count, offset, total_count):
    node_ids = jnp.arange(8, dtype=jnp.int32)[:, None]
    element_ids = offset + jnp.arange(local_count, dtype=jnp.int32)[None, :]
    at_first = node_ids == 0
    at_last = node_ids == 7
    outside = at_first & (element_ids == 0) | at_last & (element_ids == total_count - 1)
    shared = at_first & (element_ids > 0) | at_last & (element_ids < total_count - 1)
    keep_factor = jnp.where(outside, 0.0, 1.0).astype(jnp.float32)
    share_factor = jnp.where(shared, 0.5, 1.0).astype(jnp.float32)
    return (keep_factor, share_factor)

def node_masks(counts, offsets, totals):
    keep_x, share_x = edge_factors(counts[0], offsets[0], totals[0])
    keep_y, share_y = edge_factors(counts[1], offsets[1], totals[1])
    keep_z, share_z = edge_factors(counts[2], offsets[2], totals[2])
    keep_mask = (keep_x[:, None, None, :, None, None], keep_y[None, :, None, None, :, None], keep_z[None, None, :, None, None, :])
    inv_mult = (share_x[:, None, None, :, None, None], share_y[None, :, None, None, :, None], share_z[None, None, :, None, None, :])
    return (keep_mask, inv_mult)

def apply_factors(field, factors):
    return field * factors[0] * factors[1] * factors[2]

def no_neighbours(first_rim, last_rim, elem_dim):
    return (jnp.zeros_like(last_rim), jnp.zeros_like(first_rim))

def pair_sum(field, node_dim, remote):
    elem_dim = node_dim + 2
    first = jnp.take(field, 0, axis=node_dim)
    last_face = jnp.take(field, 7, axis=node_dim)
    count = first.shape[elem_dim]
    first_rim = lax.index_in_dim(first, 0, elem_dim, keepdims=False)
    last_rim = lax.index_in_dim(last_face, count - 1, elem_dim, keepdims=False)
    prev_last, next_first = remote(first_rim, last_rim, elem_dim)
    next_all = jnp.concatenate([lax.slice_in_dim(first, 1, count, axis=elem_dim), jnp.expand_dims(next_first, elem_dim)], axis=elem_dim)
    prev_all = jnp.concatenate([jnp.expand_dims(prev_last, elem_dim), lax.slice_in_dim(last_face, 0, count - 1, axis=elem_dim)], axis=elem_dim)
    new_first = first + prev_all
    new_last = last_face + next_all
    middle = lax.slice_in_dim(field, 1, 7, axis=node_dim)
    return jnp.concatenate([jnp.expand_dims(new_first, node_dim), middle, jnp.expand_dims(new_last, node_dim)], axis=node_dim)

def direct_sum(field, remote_x, remote_y):
    field = pair_sum(field, 0, remote_x)
    field = pair_sum(field, 1, remote_y)
    return pair_sum(field, 2, no_neighbours)

def stiffness_apply(field, coefficient, derivative, weight_cube):
    scaled = coefficient * weight_cube
    grad_i = contract('pi,ijkxyz->pjkxyz', derivative, field)
    grad_j = contract('qj,ijkxyz->iqkxyz', derivative, field)
    grad_k = contract('rk,ijkxyz->ijrxyz', derivative, field)
    result = contract('pi,pjkxyz->ijkxyz', derivative, stretch[0] * scaled * grad_i)
    result = result + contract('qj,iqkxyz->ijkxyz', derivative, stretch[1] * scaled * grad_j)
    return result + contract('rk,ijrxyz->ijkxyz', derivative, stretch[2] * scaled * grad_k)

def fdm_apply(field, fdm_basis, denominator):
    moved = contract('ip,ijkxyz->pjkxyz', fdm_basis, field)
    moved = contract('jq,pjkxyz->pqkxyz', fdm_basis, moved)
    moved = contract('kr,pqkxyz->pqrxyz', fdm_basis, moved)
    moved = moved * denominator
    moved = contract('ip,pqrxyz->iqrxyz', fdm_basis, moved)
    moved = contract('jq,iqrxyz->ijrxyz', fdm_basis, moved)
    return contract('kr,ijrxyz->ijkxyz', fdm_basis, moved)

def restrict_corners(weighted, linear_hat):
    corners = contract('ai,ijkxyz->ajkxyz', linear_hat, weighted)
    corners = contract('bj,ajkxyz->abkxyz', linear_hat, corners)
    return contract('ck,abkxyz->abcxyz', linear_hat, corners)

def vertex_sum(corners):
    total_grid = jnp.zeros((corners.shape[3] + 1, corners.shape[4] + 1, corners.shape[5] + 1), jnp.float32)
    for side_x in range(2):
        for side_y in range(2):
            for side_z in range(2):
                total_grid = total_grid + jnp.pad(corners[side_x, side_y, side_z], ((side_x, 1 - side_x), (side_y, 1 - side_y), (side_z, 1 - side_z)))
    return total_grid

def prolong(vertices, linear_hat):
    count_x = vertices.shape[0] - 1
    count_y = vertices.shape[1] - 1
    count_z = vertices.shape[2] - 1
    corner_vals = jnp.stack([jnp.stack([jnp.stack([vertices[side_x:side_x + count_x, side_y:side_y + count_y, side_z:side_z + count_z] for side_z in range(2)]) for side_y in range(2)]) for side_x in range(2)])
    nodal = contract('ck,abcxyz->abkxyz', linear_hat, corner_vals)
    nodal = contract('bj,abkxyz->ajkxyz', linear_hat, nodal)
    return contract('ai,ajkxyz->ijkxyz', linear_hat, nodal)

def sine_system(cells):
    wave_ints = jnp.arange(1, cells, dtype=jnp.int32)
    product_ids = wave_ints[:, None] * wave_ints[None, :] % (2 * cells)
    sine_table = math.sqrt(2.0 / cells) * jnp.sin(math.pi * product_ids.astype(jnp.float32) / cells)
    cosines = jnp.cos(math.pi * wave_ints.astype(jnp.float32) / cells)
    stiff_eig = (2.0 - 2.0 * cosines) / 2.0
    mass_eig = 2.0 * (4.0 + 2.0 * cosines) / 6.0
    return (sine_table, stiff_eig, mass_eig)

def coarse_solve(vertices):
    interior = vertices[1:-1, 1:-1, 1:-1]
    table_x, stiff_x, mass_x = sine_system(vertices.shape[0] - 1)
    table_y, stiff_y, mass_y = sine_system(vertices.shape[1] - 1)
    table_z, stiff_z, mass_z = sine_system(vertices.shape[2] - 1)
    moved = contract('mi,ijk->mjk', table_x, interior)
    moved = contract('nj,mjk->mnk', table_y, moved)
    moved = contract('ok,mnk->mno', table_z, moved)
    denominator = stretch[0] * stiff_x[:, None, None] * mass_y[None, :, None] * mass_z[None, None, :]
    denominator = denominator + stretch[1] * mass_x[:, None, None] * stiff_y[None, :, None] * mass_z[None, None, :]
    denominator = denominator + stretch[2] * mass_x[:, None, None] * mass_y[None, :, None] * stiff_z[None, None, :]
    moved = moved / denominator
    moved = contract('mi,mno->ino', table_x, moved)
    moved = contract('nj,ino->ijo', table_y, moved)
    moved = contract('ok,ijo->ijk', table_z, moved)
    return jnp.pad(moved, 1)

def reference(forcing, coefficient):
    weights, derivative, fdm_basis, eigen_values, linear_hat = spectral_tables()
    count_x, count_y, count_z = (forcing.shape[3], forcing.shape[4], forcing.shape[5])
    keep_mask, inv_mult = node_masks((count_x, count_y, count_z), (0, 0, 0), (count_x, count_y, count_z))
    weight_cube = (weights[:, None, None] * weights[None, :, None] * weights[None, None, :])[:, :, :, None, None, None]
    eigen_sum = stretch[0] * eigen_values[:, None, None] + stretch[1] * eigen_values[None, :, None] + stretch[2] * eigen_values[None, None, :]
    denominator = (1.0 / eigen_sum)[:, :, :, None, None, None]

    def assemble(field):
        return direct_sum(field, no_neighbours, no_neighbours)

    def operate(field):
        return apply_factors(assemble(stiffness_apply(field, coefficient, derivative, weight_cube)), keep_mask)

    def precondition(field):
        local_part = apply_factors(assemble(fdm_apply(field, fdm_basis, denominator)), keep_mask)
        vertices = vertex_sum(restrict_corners(apply_factors(field, inv_mult), linear_hat))
        return local_part + prolong(coarse_solve(vertices), linear_hat)

    def inner_sum(left, right):
        return jnp.sum(apply_factors(left * right, inv_mult))
    load_vec = apply_factors(assemble(forcing), keep_mask)
    pressure = jnp.zeros_like(load_vec)
    residual = load_vec
    smoothed = precondition(residual)
    direction = smoothed
    energy_now = inner_sum(residual, smoothed)
    for step_index in range(ITERS):
        image_dir = operate(direction)
        step_size = energy_now / inner_sum(direction, image_dir)
        pressure = pressure + step_size * direction
        residual = residual - step_size * image_dir
        if step_index + 1 < ITERS:
            smoothed = precondition(residual)
            energy_next = inner_sum(residual, smoothed)
            direction = smoothed + energy_next / energy_now * direction
            energy_now = energy_next
    return (pressure, residual)
```

```python
import functools
import math

import jax
import jax.numpy as jnp
import numpy as np
from jax import lax
from jax.experimental import pallas as pl
from jax.experimental.pallas import tpu as pltpu
from jax.sharding import Mesh
from jax.sharding import PartitionSpec as P

NP = 8
EX = 8
EY = 32
EZ = 128
STRETCH = (1.0, 64.0, 1.0)
CHIPS = 128
MODES = (EX - 1) * (EY - 1)
MODES_PAD = 224
F32 = jnp.float32
HIGHEST = lax.Precision.HIGHEST


def legendre(order, x):
    before, now = 1.0, x
    for n in range(2, order + 1):
        before, now = now, ((2 * n - 1) * x * now - (n - 1) * before) / n
    return now


def gll_points():
    points = [-1.0]
    for n in range(1, 7):
        x = -math.cos(math.pi * n / 7.0)
        for _ in range(60):
            x = x - (legendre(8, x) - legendre(6, x)) / (15.0 * legendre(7, x))
        points.append(x)
    points.append(1.0)
    return points


@functools.lru_cache(maxsize=None)
def spectral_tables():
    nodes = gll_points()
    values = [legendre(7, x) for x in nodes]
    w = np.array([2.0 / (56.0 * v * v) for v in values])
    deriv = np.zeros((8, 8))
    for i in range(8):
        for j in range(8):
            if i != j:
                deriv[i, j] = values[i] / (values[j] * (nodes[i] - nodes[j]))
    deriv[0, 0] = -14.0
    deriv[7, 7] = 14.0
    stiff = deriv.T @ np.diag(w) @ deriv
    stiff[0, 0] *= 2.0
    stiff[7, 7] *= 2.0
    root = 1.0 / np.sqrt(w)
    lam, vec = np.linalg.eigh(root[:, None] * stiff * root[None, :])
    basis = root[:, None] * vec
    x = np.array(nodes)
    hat = np.stack([(1.0 - x) / 2.0, (1.0 + x) / 2.0])
    hat[0, 7] = 0.0
    hat[1, 0] = 0.0
    return w, deriv, basis, lam, hat


def sine_system(cells):
    n = np.arange(1, cells)
    table = math.sqrt(2.0 / cells) * np.sin(math.pi * ((n[:, None] * n[None, :]) % (2 * cells)) / cells)
    cosines = np.cos(math.pi * n / cells)
    return table, (2.0 - 2.0 * cosines) / 2.0, 2.0 * (4.0 + 2.0 * cosines) / 6.0


@functools.lru_cache(maxsize=None)
def all_tables():
    w, deriv, basis, lam, hat = spectral_tables()
    denom = (
        STRETCH[0] * lam[:, None, None] + STRETCH[1] * lam[None, :, None] + STRETCH[2] * lam[None, None, :]
    )
    big = np.kron(np.kron(basis, basis), basis)
    local_solve = (big / denom.reshape(1, 512)) @ big.T
    corner = np.stack(
        [
            np.einsum("i,j,k->ijk", hat[a], hat[b], hat[c]).reshape(512)
            for c in range(2)
            for a in range(2)
            for b in range(2)
        ]
    )
    tx, sx, mx = sine_system(EX)
    ty, sy, my = sine_system(EY)
    tz, sz, mz = sine_system(EZ)
    vx = np.zeros((EX + 1, EX - 1))
    vx[1:-1] = tx
    vy = np.zeros((EY + 1, EY - 1))
    vy[1:-1] = ty
    vz = np.zeros((EZ + 1, EZ))
    vz[1:-1, : EZ - 1] = tz
    z_low, z_high = vz[:-1], vz[1:]
    eig = (
        STRETCH[0] * sx[:, None, None] * my[None, :, None] * mz[None, None, :]
        + STRETCH[1] * mx[:, None, None] * sy[None, :, None] * mz[None, None, :]
        + STRETCH[2] * mx[:, None, None] * my[None, :, None] * sz[None, None, :]
    )
    inv_eig = np.zeros((MODES_PAD, EZ))
    inv_eig[:MODES, : EZ - 1] = (1.0 / eig).reshape(MODES, EZ - 1)
    gather = np.zeros((2, MODES_PAD, 4 * CHIPS))
    for core in range(2):
        part = np.zeros((MODES, EX // 2, EY, 2, 2))
        for a in range(2):
            for b in range(2):
                rows_x = vx[core + a : core + a + EX - 1 : 2]
                rows_y = vy[b : b + EY]
                part[:, :, :, a, b] = np.einsum("xm,yn->mnxy", rows_x, rows_y).reshape(MODES, EX // 2, EY)
        gather[core, :MODES] = part.reshape(MODES, 4 * CHIPS)
    own_x = np.zeros((EX, 8, MODES_PAD))
    own_y = np.zeros((EY, 8, MODES_PAD))
    for side in range(2):
        for a in range(2):
            for b in range(2):
                row = side * 4 + a * 2 + b
                for x in range(EX):
                    own_x[x, row, :MODES] = np.repeat(vx[(x ^ side) + a], EY - 1)
                for y in range(EY):
                    own_y[y, row, :MODES] = np.tile(vy[y + b], EX - 1)
    lanes = np.ones((1, 128))
    roll_tables = np.zeros((18, 8, 128))
    for s in range(8):
        for r in range(8):
            roll_tables[s, r] = deriv[r, (r - s) % 8]
            roll_tables[8 + s, r] = deriv[(r - s) % 8, r]
    roll_tables[16] = hat[0][:, None] * lanes
    roll_tables[17] = hat[1][:, None] * lanes
    weight = np.einsum("i,j,k->ijk", w, w, w)[..., None] * lanes
    f = lambda t: np.asarray(t, np.float32)
    return dict(
        deriv=f(deriv),
        hat=f(hat),
        local_solve=f(local_solve),
        corner=f(corner),
        z_low=f(z_low),
        z_high=f(z_high),
        z_low_t=f(z_low.T),
        z_high_t=f(z_high.T),
        inv_eig=f(inv_eig),
        gather=f(gather),
        own_x=f(own_x),
        own_y=f(own_y),
        rolls=f(roll_tables),
        weight=f(weight),
    )


FACE = jax.ShapeDtypeStruct((8, 8, 128), F32)
NODES = jax.ShapeDtypeStruct((8, 8, 8, 128), F32)
ROWS = jax.ShapeDtypeStruct((4 * CHIPS, 128), F32)
SMALL = jax.ShapeDtypeStruct((8, 128), F32)
VMEM = pl.BlockSpec(memory_space=pltpu.VMEM)
SMEM = pl.BlockSpec(memory_space=pltpu.SMEM)


def call(body, outs, place, *args, scratch=(), name=None):
    return pl.pallas_call(
        body,
        out_shape=outs,
        in_specs=[SMEM] + [VMEM] * len(args),
        out_specs=[VMEM] * len(outs),
        scratch_shapes=list(scratch),
        name=name,
    )(place, *args)


def dot(a, b):
    return jnp.dot(a, b, precision=HIGHEST, preferred_element_type=F32)


def inner_x(place):
    return 7 * (1 - (place[0] & 1))


def inner_y(place):
    return 7 * (1 - (place[1] & 1))


def put_x_faces(place, u, inner, outer):
    at = inner_x(place)
    inner[...] = u[at]
    outer[...] = u[7 - at]


def lane_iota():
    return lax.broadcasted_iota(jnp.int32, (8, 128), 1)


def row_iota():
    return lax.broadcasted_iota(jnp.int32, (8, 128), 0)


def restrict_rows(u, corner, z_low, z_high):
    c = dot(corner[...], u[...].reshape(512, 128))
    return dot(c[0:4], z_low[...]) + dot(c[4:8], z_high[...])


def send_rows(rows, out):
    pair = jnp.concatenate([rows, rows], axis=0)
    for t in range(4 * CHIPS // 8):
        out[8 * t : 8 * t + 8] = pair


def assemble(place, u, xin, xout, yin, yout, v):
    ax, ay = inner_x(place), inner_y(place)
    keep_x = jnp.where((place[0] == 0) | (place[0] == EX - 1), 0.0, 1.0).astype(F32)
    keep_y = jnp.where((place[1] == 0) | (place[1] == EY - 1), 0.0, 1.0).astype(F32)
    v[...] = u[...]
    v[ax] = v[ax] + xin[...]
    v[7 - ax] = (v[7 - ax] + xout[...]) * keep_x
    for i in range(8):
        v[i, ay] = v[i, ay] + yin[i]
        v[i, 7 - ay] = (v[i, 7 - ay] + yout[i]) * keep_y
    v[7 - ax] = v[7 - ax] * keep_x
    lane, row = lane_iota(), row_iota()
    first, last = row == 0, row == 7
    keep_z = jnp.where((first & (lane == 0)) | (last & (lane == 127)), 0.0, 1.0).astype(F32)
    for i in range(8):
        for j in range(8):
            t = v[i, j]
            from_prev = pltpu.roll(pltpu.roll(t, 1, 1), 1, 0)
            from_next = pltpu.roll(pltpu.roll(t, 127, 1), 7, 0)
            t = t + jnp.where(first, from_prev, 0.0) + jnp.where(last, from_next, 0.0)
            v[i, j] = t * keep_z


def stiffness(u, cw, rolls, out):
    deriv = all_tables()["deriv"]
    for j in range(8):
        q = []
        vals = [u[i, j] for i in range(8)]
        for p in range(8):
            g = float(deriv[p, 0]) * vals[0]
            for i in range(1, 8):
                g = g + float(deriv[p, i]) * vals[i]
            q.append(g * cw[p, j])
        for i in range(8):
            r = float(deriv[0, i]) * q[0]
            for p in range(1, 8):
                r = r + float(deriv[p, i]) * q[p]
            out[i, j] = r
    for i in range(8):
        q = []
        vals = [u[i, j] for j in range(8)]
        for p in range(8):
            g = float(deriv[p, 0]) * vals[0]
            for j in range(1, 8):
                g = g + float(deriv[p, j]) * vals[j]
            q.append(g * (STRETCH[1] * cw[i, p]))
        for j in range(8):
            r = float(deriv[0, j]) * q[0]
            for p in range(1, 8):
                r = r + float(deriv[p, j]) * q[p]
            out[i, j] = out[i, j] + r
    for i in range(8):
        for j in range(8):
            t = u[i, j]
            g = rolls[0] * t
            for s in range(1, 8):
                g = g + rolls[s] * pltpu.roll(t, s, 0)
            q = g * cw[i, j]
            r = rolls[8] * q
            for s in range(1, 8):
                r = r + rolls[8 + s] * pltpu.roll(q, s, 0)
            out[i, j] = out[i, j] + r


def prolong_add(coarse, rolls, z_low_t, z_high_t, v):
    hat = all_tables()["hat"]
    low = dot(coarse, z_low_t[...])
    high = dot(coarse, z_high_t[...])
    h0, h1 = rolls[16], rolls[17]
    line = [h0 * low[r : r + 1] + h1 * high[r : r + 1] for r in range(4)]
    for j in range(8):
        near = float(hat[0, j]) * line[0] + float(hat[1, j]) * line[1]
        far = float(hat[0, j]) * line[2] + float(hat[1, j]) * line[3]
        for i in range(8):
            v[i, j] = v[i, j] + (float(hat[0, i]) * near + float(hat[1, i]) * far)


def total(a, b):
    return jnp.sum(a[...] * b[...], keepdims=True).reshape(1, 1)


def k_faces(place, u, inner, outer):
    put_x_faces(place, u, inner, outer)


def k_restrict(place, u, corner, z_low, z_high, rows):
    send_rows(restrict_rows(u, corner, z_low, z_high), rows)


def k_weight(place, coefficient, weight, cw):
    cw[...] = coefficient[...] * weight[...]


def k_y_faces(place, u, xin, xout, inner, outer):
    ax, ay = inner_x(place), inner_y(place)
    for face, at in ((inner, ay), (outer, 7 - ay)):
        for i in range(8):
            face[i] = u[i, at]
        face[ax] = face[ax] + xin[at]
        face[7 - ax] = face[7 - ax] + xout[at]


def k_local_solve(place, u, xin, xout, yin, yout, solve, v, h, hin, hout):
    assemble(place, u, xin, xout, yin, yout, v)
    h[...] = dot(solve[...], v[...].reshape(512, 128)).reshape(8, 8, 8, 128)
    put_x_faces(place, h, hin, hout)


def k_coarse(place, got, gather, inv_eig, own_x, own_y, out):
    modes = dot(gather[place[2]], got[...]) * inv_eig[...]
    mine = dot(own_x[place[0]] * own_y[place[1]], modes)
    sums = jnp.sum(got[...].reshape(4 * CHIPS // 8, 8, 128), axis=0)
    sums = sums + pltpu.roll(sums, 4, 0)
    out[...] = jnp.where(lane_iota() == 127, sums, mine)


def k_first(
    place, h, xin, xout, yin, yout, mine, theirs, f, cw, rolls, z_low_t, z_high_t, corner, z_low, z_high,
    s, g, gin, gout, rows,
):
    assemble(place, h, xin, xout, yin, yout, s)
    prolong_add(mine[0:4] + theirs[4:8], rolls, z_low_t, z_high_t, s)
    stiffness(s, cw, rolls, g)
    put_x_faces(place, g, gin, gout)
    modes = restrict_rows(g, corner, z_low, z_high)
    lane, row = lax.broadcasted_iota(jnp.int32, (4, 128), 1), lax.broadcasted_iota(jnp.int32, (4, 128), 0)
    sums = jnp.where(row == 0, total(f, s), jnp.where(row == 1, total(s, g), 0.0))
    send_rows(jnp.where(lane == 127, sums, modes), rows)


def k_second(
    place, h, xin, xout, yin, yout, mine, theirs, f, s0, g0, cw, rolls, z_low_t, z_high_t,
    s1, h1, gin, gout, rows, scalars, t,
):
    assemble(place, h, xin, xout, yin, yout, t)
    coarse = mine[0:4] + theirs[4:8]
    prolong_add(coarse, rolls, z_low_t, z_high_t, t)
    lane4 = lax.broadcasted_iota(jnp.int32, (4, 128), 1)
    known = jnp.sum(jnp.where(lane4 == 127, coarse, 0.0), axis=1, keepdims=True)
    energy, curve = known[0:1], known[1:2]
    step = energy / curve
    s1[...] = s0[...] - step * t[...]
    stiffness(s1, cw, rolls, h1)
    put_x_faces(place, h1, gin, gout)
    fresh = jnp.sum(s1[...] * (f[...] - step * g0[...]), keepdims=True).reshape(1, 1)
    sums = (fresh, total(s1, h1), total(s1, g0), total(s0, h1))
    lane = lane_iota()
    row = jnp.zeros((8, 128), F32)
    for n, value in enumerate(sums):
        row = jnp.where(lane == n, value, row)
    for n in range(2 * CHIPS // 8):
        rows[8 * n : 8 * n + 8] = row
    lane = lane_iota()
    scalars[...] = jnp.where(lane == 0, energy, jnp.where(lane == 1, curve, step))


def k_last(place, h, xin, xout, yin, yout, got, scalars, s0, s1, b, w, p, r):
    sums = jnp.sum(got[...], axis=0, keepdims=True)
    fresh, s1h1, s1g0, s0h1 = (sums[:, n : n + 1] for n in range(4))
    energy, curve, step0 = (scalars[0:1, n : n + 1] for n in range(3))
    beta = fresh / energy
    step1 = fresh / (s1h1 + beta * (s1g0 + s0h1) + beta * beta * curve)
    assemble(place, h, xin, xout, yin, yout, r)
    p[...] = step0 * s0[...] + step1 * (s1[...] + beta * s0[...])
    r[...] = (b[...] - step0 * w[...]) - step1 * (r[...] + beta * w[...])


CHIP_AXES = ("x", "y", "z")
ALL_AXES = ("x", "c", "y", "z")
SWAP = [(0, 1), (1, 0)]


def pairs(count, start):
    out = []
    for n in range(start, count - 1, 2):
        out += [(n, n + 1), (n + 1, n)]
    return out


def swap_x(inner, outer):
    return (
        lax.ppermute(inner, "c", SWAP),
        lax.ppermute(outer, ("x", "c"), pairs(EX, 1)),
    )


def swap_y(inner, outer):
    return (
        lax.ppermute(inner, ("y", "z"), pairs(EY, 0)),
        lax.ppermute(outer, ("y", "z"), pairs(EY, 1)),
    )


def share(rows):
    got = lax.all_to_all(rows.reshape(CHIPS, 4, 128), CHIP_AXES, 0, 0)
    return got.reshape(4 * CHIPS, 128)


def on_device(forcing, coefficient):
    tables = all_tables()
    tab = lambda *names: [jnp.asarray(tables[n]) for n in names]
    f = forcing.reshape(8, 8, 8, 128)
    coef = coefficient.reshape(8, 8, 8, 128)
    px = lax.axis_index(("x", "c")).astype(jnp.int32)
    py = lax.axis_index(("y", "z")).astype(jnp.int32)
    n = jnp.arange(4, dtype=jnp.int32)
    place = jnp.where(n == 0, px, jnp.where(n == 1, py, px & 1))

    def halo(u, inner, outer):
        xs = swap_x(inner, outer)
        ys = swap_y(*call(k_y_faces, (FACE, FACE), place, u, *xs, name="yfaces"))
        return xs + ys

    def coarse(rows):
        got = share(rows)
        mine = call(
            k_coarse, (SMALL,), place, got, *tab("gather", "inv_eig", "own_x", "own_y"), name="coarse"
        )[0]
        return mine, lax.ppermute(mine, "c", SWAP)

    def local(u, sides):
        return call(
            k_local_solve, (NODES, NODES, FACE, FACE), place, u, *sides, *tab("local_solve"), name="solve"
        )

    faces = call(k_faces, (FACE, FACE), place, f, name="faces")
    rows = call(k_restrict, (ROWS,), place, f, *tab("corner", "z_low", "z_high"), name="restrict")[0]
    cw = call(k_weight, (NODES,), place, coef, *tab("weight"), name="weight")[0]
    c0 = coarse(rows)
    b, h, hin, hout = local(f, halo(f, *faces))
    s0, g0, gin, gout, rows = call(
        k_first, (NODES, NODES, FACE, FACE, ROWS), place, h, *halo(h, hin, hout), *c0, f, cw,
        *tab("rolls", "z_low_t", "z_high_t", "corner", "z_low", "z_high"), name="first",
    )
    c1 = coarse(rows)
    w, h, hin, hout = local(g0, halo(g0, gin, gout))
    s1, h1, gin, gout, rows, scalars = call(
        k_second,
        (NODES, NODES, FACE, FACE, jax.ShapeDtypeStruct((2 * CHIPS, 128), F32), SMALL),
        place, h, *halo(h, hin, hout), *c1, f, s0, g0, cw, *tab("rolls", "z_low_t", "z_high_t"),
        scratch=(pltpu.VMEM((8, 8, 8, 128), F32),), name="second",
    )
    got = lax.all_to_all(rows.reshape(2 * CHIPS, 1, 128), ALL_AXES, 0, 0).reshape(2 * CHIPS, 128)
    p, r = call(
        k_last, (NODES, NODES), place, h1, *halo(h1, gin, gout), got, scalars, s0, s1, b, w, name="last"
    )
    return p.reshape(forcing.shape), r.reshape(forcing.shape)


def solution(mesh):
    fine = Mesh(mesh.devices.reshape(4, 2, 4, 8), ALL_AXES)
    spec = P(None, None, None, ("x", "c"), ("y", "z"), None)
    return jax.shard_map(
        on_device, mesh=fine, in_specs=(spec, spec), out_specs=(spec, spec), check_vma=False
    )
```

```python
import functools
import math

import jax
import jax.numpy as jnp
import numpy as np
from jax import lax
from jax.experimental import pallas as pl
from jax.experimental.pallas import tpu as pltpu
from jax.sharding import Mesh
from jax.sharding import PartitionSpec as P


EX = 8
EY = 32
EZ = 128
STRETCH = (1.0, 64.0, 1.0)
CHIPS = 128
MODES = (EX - 1) * (EY - 1)
MODES_PAD = 224
F32 = jnp.float32
BF16 = jnp.bfloat16


def legendre(order, x):
    before, now = 1.0, x
    for n in range(2, order + 1):
        before, now = now, ((2 * n - 1) * x * now - (n - 1) * before) / n
    return now


def gll_points():
    points = [-1.0]
    for n in range(1, 7):
        x = -math.cos(math.pi * n / 7.0)
        for _ in range(60):
            x = x - (legendre(8, x) - legendre(6, x)) / (15.0 * legendre(7, x))
        points.append(x)
    points.append(1.0)
    return points


@functools.lru_cache(maxsize=None)
def spectral_tables():
    nodes = gll_points()
    values = [legendre(7, x) for x in nodes]
    w = np.array([2.0 / (56.0 * v * v) for v in values])
    deriv = np.zeros((8, 8))
    for i in range(8):
        for j in range(8):
            if i != j:
                deriv[i, j] = values[i] / (values[j] * (nodes[i] - nodes[j]))
    deriv[0, 0] = -14.0
    deriv[7, 7] = 14.0
    stiff = deriv.T @ np.diag(w) @ deriv
    stiff[0, 0] *= 2.0
    stiff[7, 7] *= 2.0
    root = 1.0 / np.sqrt(w)
    lam, vec = np.linalg.eigh(root[:, None] * stiff * root[None, :])
    basis = root[:, None] * vec
    x = np.array(nodes)
    hat = np.stack([(1.0 - x) / 2.0, (1.0 + x) / 2.0])
    hat[0, 7] = 0.0
    hat[1, 0] = 0.0
    return w, deriv, basis, lam, hat


def sine_system(cells):
    n = np.arange(1, cells)
    table = math.sqrt(2.0 / cells) * np.sin(math.pi * ((n[:, None] * n[None, :]) % (2 * cells)) / cells)
    cosines = np.cos(math.pi * n / cells)
    return table, (2.0 - 2.0 * cosines) / 2.0, 2.0 * (4.0 + 2.0 * cosines) / 6.0


@functools.lru_cache(maxsize=None)
def all_tables():
    w, deriv, basis, lam, hat = spectral_tables()
    denom = (
        STRETCH[0] * lam[:, None, None] + STRETCH[1] * lam[None, :, None] + STRETCH[2] * lam[None, None, :]
    )
    big = np.kron(np.kron(basis, basis), basis)
    full = ((big / denom.reshape(1, 512)) @ big.T).reshape(8, 8, 8, 8, 8, 8)
    local_solve = []
    for si in (1.0, -1.0):
        for sj in (1.0, -1.0):
            t = full[:4, :4]
            t = 0.5 * (t[:, :, :, :4] + si * t[:, :, :, 7:3:-1])
            t = 0.5 * (t[:, :, :, :, :4] + sj * t[:, :, :, :, 7:3:-1])
            local_solve.append(t.reshape(128, 128))
    local_solve = np.stack(local_solve)
    tx, sx, mx = sine_system(EX)
    ty, sy, my = sine_system(EY)
    tz, sz, mz = sine_system(EZ)
    vx = np.zeros((EX + 1, EX - 1))
    vx[1:-1] = tx
    vy = np.zeros((EY + 1, EY - 1))
    vy[1:-1] = ty
    vz = np.zeros((EZ + 1, EZ))
    vz[1:-1, : EZ - 1] = tz
    z_low, z_high = vz[:-1], vz[1:]
    eig = (
        STRETCH[0] * sx[:, None, None] * my[None, :, None] * mz[None, None, :]
        + STRETCH[1] * mx[:, None, None] * sy[None, :, None] * mz[None, None, :]
        + STRETCH[2] * mx[:, None, None] * my[None, :, None] * sz[None, None, :]
    )
    inv_eig = np.zeros((MODES_PAD, EZ))
    inv_eig[:MODES, : EZ - 1] = (1.0 / eig).reshape(MODES, EZ - 1)
    part = np.zeros((MODES, EX // 2, EY, 2, 2))
    for a in range(2):
        for b in range(2):
            rows_x = vx[a : a + EX - 1 : 2]
            rows_y = vy[b : b + EY]
            part[:, :, :, a, b] = np.einsum("xm,yn->mnxy", rows_x, rows_y).reshape(MODES, EX // 2, EY)
    gather = np.zeros((MODES_PAD, 4 * CHIPS))
    gather[:MODES] = part.reshape(MODES, 4 * CHIPS)
    flip = np.array([1.0 if m % 2 == 0 else -1.0 for m in range(EX - 1)])
    own_x = np.zeros((EX, 8, MODES_PAD))
    for x in range(EX):
        for row in range(8):
            side, a = row // 4, row // 2 % 2
            sign = flip if x % 2 else 1.0
            own_x[x, row, :MODES] = np.repeat(sign * vx[(x ^ side) + a], EY - 1)
    own_y = np.zeros((EY + 8, MODES_PAD))
    own_y[: EY + 1, :MODES] = np.tile(vy, (1, EX - 1))
    lanes = np.ones((1, 128))
    roll_tables = np.zeros((19, 8, 128))
    for s in range(8):
        for r in range(8):
            roll_tables[s, r] = deriv[r, (r - s) % 8]
            roll_tables[8 + s, r] = deriv[(r - s) % 8, r]
    roll_tables[16] = hat[0][:, None] * lanes
    roll_tables[17] = hat[1][:, None] * lanes
    roll_tables[18] = w[:, None] * lanes
    f = lambda t: np.asarray(t, np.float32)

    def split(t):
        high = t.astype(BF16)
        return np.stack([high, (t - high.astype(np.float64)).astype(BF16)])

    return dict(
        deriv=f(deriv),
        hat=f(hat),
        local_solve=split(local_solve),
        z_in=split(np.concatenate([z_low, z_high], axis=1)),
        z_out=split(np.concatenate([z_low.T, z_high.T], axis=1)),
        inv_eig=f(inv_eig),
        gather=split(gather),
        own_x=f(own_x),
        own_y=f(own_y),
        rolls=f(roll_tables),
        weight=w,
    )


FACE = jax.ShapeDtypeStruct((8, 8, 128), F32)
FACES = (FACE,) * 4
NODES = jax.ShapeDtypeStruct((8, 8, 8, 128), F32)
ROWS = jax.ShapeDtypeStruct((4 * CHIPS, 128), F32)
SMALL = jax.ShapeDtypeStruct((8, 128), F32)
VMEM = pl.BlockSpec(memory_space=pltpu.VMEM)
SMEM = pl.BlockSpec(memory_space=pltpu.SMEM)


def call(body, outs, place, *args, scratch=(), specs=None):
    return pl.pallas_call(
        body,
        out_shape=outs,
        in_specs=[SMEM] + (specs or [VMEM] * len(args)),
        out_specs=[VMEM] * len(outs),
        scratch_shapes=list(scratch),
        compiler_params=pltpu.CompilerParams(vmem_limit_bytes=12 << 20),
    )(place, *args)


def parts(x):
    high = x.astype(jnp.bfloat16)
    return high, (x - high.astype(F32)).astype(jnp.bfloat16)


def dot(a, b):
    return jnp.dot(a, b, preferred_element_type=F32)


def table_dot(table, x):
    high, low = parts(x)
    return dot(table[0], high) + (dot(table[0], low) + dot(table[1], high))


def dot_table(x, table):
    high, low = parts(x)
    first = dot(jnp.concatenate([high, low], axis=0), table[0])
    return first[0:8] + (first[8:16] + dot(high, table[1]))


def inner_x(place):
    return 7 * (1 - (place[0] & 1))


def inner_y(place):
    return 7 * (1 - (place[1] & 1))


def put_faces(place, u, faces):
    xin, xout, yin, yout = faces
    ax, ay = inner_x(place), inner_y(place)
    xin[...] = u[ax]
    xout[...] = u[7 - ax]
    for i in range(8):
        yin[i] = u[i, ay]
        yout[i] = u[i, 7 - ay]


def lane_iota():
    return lax.broadcasted_iota(jnp.int32, (8, 128), 1)


def row_iota():
    return lax.broadcasted_iota(jnp.int32, (8, 128), 0)


def weighted(coefs, vals):
    out = None
    for c, v in zip(coefs, vals):
        if c != 0.0:
            t = v if c == 1.0 else float(c) * v
            out = t if out is None else out + t
    return out


def restrict_rows(place, u, rolls, z_in):
    hat = all_tables()["hat"]
    near = [[weighted(hat[b], [u[i, j] for j in range(8)]) for i in range(8)] for b in range(2)]
    corner = [[weighted(hat[a], near[b]) for b in range(2)] for a in range(2)]
    row = row_iota()
    odd = (place[0] & 1) == 1
    out = jnp.zeros((8, 128), F32)
    for c in range(2):
        for a in range(2):
            for b in range(2):
                line = jnp.sum(rolls[16 + c] * corner[a][b], axis=0, keepdims=True)
                at = jnp.where(odd, 4 * c + 2 * (1 - a) + b, 4 * c + 2 * a + b)
                out = jnp.where(row == at, line, out)
    modes = dot_table(out, z_in)
    return modes[0:4, 0:128] + modes[4:8, 128:256]


def send_rows(rows, out):
    pair = jnp.concatenate([rows, rows], axis=0)
    for t in range(4 * CHIPS // 8):
        out[8 * t : 8 * t + 8] = pair


def assemble(place, u, xin, xout, yin, yout, v):
    ax, ay = inner_x(place), inner_y(place)
    keep_x = jnp.where((place[0] == 0) | (place[0] == EX - 1), 0.0, 1.0).astype(F32)
    keep_y = jnp.where((place[1] == 0) | (place[1] == EY - 1), 0.0, 1.0).astype(F32)
    v[...] = u[...]
    v[ax] = v[ax] + xin[...]
    v[7 - ax] = (v[7 - ax] + xout[...]) * keep_x
    for i in range(8):
        v[i, ay] = v[i, ay] + yin[i]
        v[i, 7 - ay] = (v[i, 7 - ay] + yout[i]) * keep_y
    v[7 - ax] = v[7 - ax] * keep_x
    lane, row = lane_iota(), row_iota()
    first, last = row == 0, row == 7
    keep_z = jnp.where((first & (lane == 0)) | (last & (lane == 127)), 0.0, 1.0).astype(F32)
    for i in range(8):
        for j in range(8):
            t = v[i, j]
            from_prev = pltpu.roll(pltpu.roll(t, 1, 1), 1, 0)
            from_next = pltpu.roll(pltpu.roll(t, 127, 1), 7, 0)
            t = t + jnp.where(first, from_prev, 0.0) + jnp.where(last, from_next, 0.0)
            v[i, j] = t * keep_z


def lines(vals, weights, deriv):
    even = 0.5 * (deriv[:4, :4] + deriv[:4, 7:3:-1])
    odd = 0.5 * (deriv[:4, :4] - deriv[:4, 7:3:-1])
    sums = [vals[i] + vals[7 - i] for i in range(4)]
    difs = [vals[i] - vals[7 - i] for i in range(4)]
    u, v = [], []
    for p in range(4):
        e, o = weighted(even[p], sums), weighted(odd[p], difs)
        q, r = (o + e) * weights[p], (o - e) * weights[7 - p]
        u.append(q - r)
        v.append(q + r)
    out = [None] * 8
    for i in range(4):
        e, o = weighted(even[:, i], u), weighted(odd[:, i], v)
        out[i], out[7 - i] = e + o, e - o
    return out


def stiffness(u, cw, rolls, out):
    deriv = all_tables()["deriv"].astype(np.float64)
    for j in range(8):
        r = lines([u[i, j] for i in range(8)], [cw[i, j] for i in range(8)], deriv)
        for i in range(8):
            out[i, j] = r[i]
    for i in range(8):
        r = lines([u[i, j] for j in range(8)], [cw[i, j] for j in range(8)], deriv)
        for j in range(8):
            t = u[i, j]
            g = rolls[0] * t
            for s in range(1, 8):
                g = g + rolls[s] * pltpu.roll(t, s, 0)
            q = g * cw[i, j]
            k = rolls[8] * q
            for s in range(1, 8):
                k = k + rolls[8 + s] * pltpu.roll(q, s, 0)
            out[i, j] = out[i, j] + (STRETCH[1] * r[j] + k)


def prolong_add(coarse, rolls, z_out, v):
    hat = all_tables()["hat"]
    both = dot_table(coarse, z_out)
    low, high = both[:, 0:128], both[:, 128:256]
    h0, h1 = rolls[16], rolls[17]
    line = [h0 * low[r : r + 1] + h1 * high[r : r + 1] for r in range(4)]
    for j in range(8):
        near = float(hat[0, j]) * line[0] + float(hat[1, j]) * line[1]
        far = float(hat[0, j]) * line[2] + float(hat[1, j]) * line[3]
        for i in range(8):
            v[i, j] = v[i, j] + (float(hat[0, i]) * near + float(hat[1, i]) * far)


def total(a, b):
    return jnp.sum(a[...] * b[...], keepdims=True).reshape(1, 1)


def k_faces(place, u, xin, xout, yin, yout, sems):
    ax, ay = inner_x(place), inner_y(place)
    sources = (u.at[ax], u.at[7 - ax], u.at[:, ay], u.at[:, 7 - ay])
    copies = [
        pltpu.make_async_copy(source, face, sems.at[n])
        for n, (source, face) in enumerate(zip(sources, (xin, xout, yin, yout)))
    ]
    for copy in copies:
        copy.start()
    for copy in copies:
        copy.wait()


def k_restrict(place, u, coefficient, rolls, z_in, rows, cw):
    send_rows(restrict_rows(place, u, rolls, z_in), rows)
    w = all_tables()["weight"]
    for i in range(8):
        for j in range(8):
            cw[i, j] = coefficient[i, j] * (float(w[i] * w[j]) * rolls[18])


def k_local_solve(place, u, xin, xout, yin, yout, solve, v, h, *faces):
    assemble(place, u, xin, xout, yin, yout, v)
    out = []
    for si in range(2):
        for sj in range(2):
            block = []
            for i in range(4):
                for j in range(4):
                    near, far = v[i, j], v[7 - i, j]
                    near_j, far_j = v[i, 7 - j], v[7 - i, 7 - j]
                    left = near - far if si else near + far
                    right = near_j - far_j if si else near_j + far_j
                    block.append(left - right if sj else left + right)
            high, low = parts(jnp.concatenate(block, axis=0))
            t, t_low = solve[0, 2 * si + sj], solve[1, 2 * si + sj]
            out.append((dot(t, high) + (dot(t, low) + dot(t_low, high))).reshape(4, 4, 8, 128))
    for i in range(4):
        for j in range(4):
            pp, pm, mp, mm = (block[i, j] for block in out)
            a, b, c, d = pp + pm, pp - pm, mp + mm, mp - mm
            h[i, j] = a + c
            h[7 - i, j] = a - c
            h[i, 7 - j] = b + d
            h[7 - i, 7 - j] = b - d
    put_faces(place, h, faces)


def k_coarse(place, got, gather, inv_eig, own_x, own_y, out):
    core = place[2]
    size = CHIPS
    blocks = [got[pl.ds(pl.multiple_of(size * (n + core * (3 - 2 * n)), size), size)] for n in range(4)]
    modes = table_dot(gather, jnp.concatenate(blocks, axis=0)) * inv_eig[...]
    row = lax.broadcasted_iota(jnp.int32, (8, MODES_PAD), 0)
    low, high = own_y[pl.ds(place[1], 1)], own_y[pl.ds(place[1] + 1, 1)]
    own = own_x[place[0]] * jnp.where((row & 1) == 0, low, high)
    own_high, own_low = parts(own)
    high, low = parts(modes)
    first = dot(jnp.concatenate([own_high, own_low], axis=0), high)
    mine = first[0:8] + (first[8:16] + dot(own_high, low))
    sums = jnp.sum(got[...].reshape(4 * CHIPS // 8, 8, 128), axis=0)
    sums = sums + pltpu.roll(sums, 4, 0)
    out[...] = jnp.where(lane_iota() == 127, sums, mine)


def both_halves(mine, theirs):
    return mine[...] + pltpu.roll(theirs[...], 4, 0)


def k_first(
    place, h, xin, xout, yin, yout, mine, theirs, f, cw, rolls, z_out, z_in, s, g, rows, *faces
):
    assemble(place, h, xin, xout, yin, yout, s)
    prolong_add(both_halves(mine, theirs), rolls, z_out, s)
    stiffness(s, cw, rolls, g)
    put_faces(place, g, faces)
    modes = restrict_rows(place, g, rolls, z_in)
    lane, row = lax.broadcasted_iota(jnp.int32, (4, 128), 1), lax.broadcasted_iota(jnp.int32, (4, 128), 0)
    sums = jnp.where(row == 0, total(f, s), jnp.where(row == 1, total(s, g), 0.0))
    send_rows(jnp.where(lane == 127, sums, modes), rows)


def k_second(
    place, h, xin, xout, yin, yout, mine, theirs, f, s0, g0, cw, rolls, z_out,
    s1, h1, rows, scalars, *rest,
):
    faces, t = rest[:4], rest[4]
    assemble(place, h, xin, xout, yin, yout, t)
    coarse = both_halves(mine, theirs)
    prolong_add(coarse, rolls, z_out, t)
    lane = lane_iota()
    known = jnp.sum(jnp.where(lane == 127, coarse, 0.0), axis=1, keepdims=True)
    energy, curve = known[0:1], known[1:2]
    step = energy / curve
    s1[...] = s0[...] - step * t[...]
    stiffness(s1, cw, rolls, h1)
    put_faces(place, h1, faces)
    fresh = jnp.sum(s1[...] * (f[...] - step * g0[...]), keepdims=True).reshape(1, 1)
    sums = (fresh, total(s1, h1), total(s1, g0), total(s0, h1))
    row = jnp.zeros((8, 128), F32)
    for n, value in enumerate(sums):
        row = jnp.where(lane == n, value, row)
    for n in range(2 * CHIPS // 8):
        rows[8 * n : 8 * n + 8] = row
    scalars[...] = jnp.where(lane == 0, energy, jnp.where(lane == 1, curve, step))


def k_last(place, h, xin, xout, yin, yout, got, scalars, s0, s1, b, w, p, r):
    sums = jnp.sum(got[...], axis=0, keepdims=True)
    fresh, s1h1, s1g0, s0h1 = (sums[:, n : n + 1] for n in range(4))
    energy, curve, step0 = (scalars[0:1, n : n + 1] for n in range(3))
    beta = fresh / energy
    step1 = fresh / (s1h1 + beta * (s1g0 + s0h1) + beta * beta * curve)
    assemble(place, h, xin, xout, yin, yout, r)
    p[...] = step0 * s0[...] + step1 * (s1[...] + beta * s0[...])
    r[...] = (b[...] - step0 * w[...]) - step1 * (r[...] + beta * w[...])


CHIP_AXES = ("x", "y", "z")
ALL_AXES = ("x", "c", "y", "z")
SWAP = [(0, 1), (1, 0)]


def pairs(count, start):
    out = []
    for n in range(start, count, 2):
        out += [(n, (n + 1) % count), ((n + 1) % count, n)]
    return out


def swap_x(inner, outer):
    far = lax.ppermute(outer, ("x", "c"), pairs(EX, 1))
    near = lax.ppermute(inner, "c", SWAP)
    return near, far


def swap_y(inner, outer):
    far = lax.ppermute(outer, ("y", "z"), pairs(EY, 1))
    near = lax.ppermute(inner, ("y", "z"), pairs(EY, 0))
    return near, far


def share(rows):
    got = lax.all_to_all(rows.reshape(CHIPS, 4, 128), CHIP_AXES, 0, 0)
    return got.reshape(4 * CHIPS, 128)


def on_device(forcing, coefficient):
    tables = all_tables()
    tab = lambda *names: [jnp.asarray(tables[n]) for n in names]
    f = forcing.reshape(8, 8, 8, 128)
    coef = coefficient.reshape(8, 8, 8, 128)
    px = lax.axis_index(("x", "c")).astype(jnp.int32)
    py = lax.axis_index(("y", "z")).astype(jnp.int32)
    n = jnp.arange(4, dtype=jnp.int32)
    place = jnp.where(n == 0, px, jnp.where(n == 1, py, px & 1))

    inside = jnp.arange(8, dtype=jnp.int32)[:, None, None] == 7 * (1 - (px & 1))
    outside = jnp.arange(8, dtype=jnp.int32)[:, None, None] == 7 * (px & 1)
    even = (py & 1) == 0

    def y_face(raw, last, xin, xout):
        near = jnp.where(last, xin[7], xin[0])[None]
        far = jnp.where(last, xout[7], xout[0])[None]
        return raw + jnp.where(inside, near, jnp.where(outside, far, 0.0))

    def halo(xin, xout, yin, yout):
        xs = swap_x(xin, xout)
        ys = swap_y(y_face(yin, even, *xs), y_face(yout, ~even, *xs))
        return xs + ys

    def coarse(rows):
        got = share(rows)
        mine = call(k_coarse, (SMALL,), place, got, *tab("gather", "inv_eig", "own_x", "own_y"))[0]
        return mine, lax.ppermute(mine, "c", SWAP)

    def local(u, sides):
        out = call(k_local_solve, (NODES, NODES) + FACES, place, u, *sides, *tab("local_solve"))
        return out[0], out[1], out[2:]

    faces = call(
        k_faces, FACES, place, f,
        specs=[pl.BlockSpec(memory_space=pl.ANY)], scratch=(pltpu.SemaphoreType.DMA((4,)),),
    )
    rows, cw = call(k_restrict, (ROWS, NODES), place, f, coef, *tab("rolls", "z_in"))
    c0 = coarse(rows)
    b, h, faces = local(f, halo(*faces))
    s0, g0, rows, *faces1 = call(
        k_first, (NODES, NODES, ROWS) + FACES, place, h, *halo(*faces), *c0, f, cw,
        *tab("rolls", "z_out", "z_in"),
    )
    c1 = coarse(rows)
    w, h, faces = local(g0, halo(*faces1))
    s1, h1, rows, scalars, *faces1 = call(
        k_second,
        (NODES, NODES, jax.ShapeDtypeStruct((2 * CHIPS, 128), F32), SMALL) + FACES,
        place, h, *halo(*faces), *c1, f, s0, g0, cw, *tab("rolls", "z_out"),
        scratch=(pltpu.VMEM((8, 8, 8, 128), F32),),
    )
    got = lax.all_to_all(rows.reshape(2 * CHIPS, 1, 128), ALL_AXES, 0, 0).reshape(2 * CHIPS, 128)
    sides = halo(*faces1)
    p, r = call(k_last, (NODES, NODES), place, h1, *sides, got, scalars, s0, s1, b, w)
    return p.reshape(forcing.shape), r.reshape(forcing.shape)


def solution(mesh):
    fine = Mesh(mesh.devices.reshape(4, 2, 4, 8), ALL_AXES)
    spec = P(None, None, None, ("x", "c"), ("y", "z"), None)
    return jax.shard_map(
        on_device, mesh=fine, in_specs=(spec, spec), out_specs=(spec, spec), check_vma=False
    )
```

```python
import functools
import math

import jax
import jax.numpy as jnp
import numpy as np
from jax import lax
from jax.experimental import pallas as pl
from jax.experimental.pallas import tpu as pltpu
from jax.sharding import Mesh
from jax.sharding import PartitionSpec as P


EX = 8
EY = 32
EZ = 128
STRETCH = (1.0, 64.0, 1.0)
CHIPS = 128
MODES = (EX - 1) * (EY - 1)
MODES_PAD = 224
F32 = jnp.float32
BF16 = jnp.bfloat16


def legendre(order, x):
    before, now = 1.0, x
    for n in range(2, order + 1):
        before, now = now, ((2 * n - 1) * x * now - (n - 1) * before) / n
    return now


def gll_points():
    points = [-1.0]
    for n in range(1, 7):
        x = -math.cos(math.pi * n / 7.0)
        for _ in range(60):
            x = x - (legendre(8, x) - legendre(6, x)) / (15.0 * legendre(7, x))
        points.append(x)
    points.append(1.0)
    return points


@functools.lru_cache(maxsize=None)
def spectral_tables():
    nodes = gll_points()
    values = [legendre(7, x) for x in nodes]
    w = np.array([2.0 / (56.0 * v * v) for v in values])
    deriv = np.zeros((8, 8))
    for i in range(8):
        for j in range(8):
            if i != j:
                deriv[i, j] = values[i] / (values[j] * (nodes[i] - nodes[j]))
    deriv[0, 0] = -14.0
    deriv[7, 7] = 14.0
    stiff = deriv.T @ np.diag(w) @ deriv
    stiff[0, 0] *= 2.0
    stiff[7, 7] *= 2.0
    root = 1.0 / np.sqrt(w)
    lam, vec = np.linalg.eigh(root[:, None] * stiff * root[None, :])
    basis = root[:, None] * vec
    x = np.array(nodes)
    hat = np.stack([(1.0 - x) / 2.0, (1.0 + x) / 2.0])
    hat[0, 7] = 0.0
    hat[1, 0] = 0.0
    return w, deriv, basis, lam, hat


def sine_system(cells):
    n = np.arange(1, cells)
    table = math.sqrt(2.0 / cells) * np.sin(math.pi * ((n[:, None] * n[None, :]) % (2 * cells)) / cells)
    cosines = np.cos(math.pi * n / cells)
    return table, (2.0 - 2.0 * cosines) / 2.0, 2.0 * (4.0 + 2.0 * cosines) / 6.0


@functools.lru_cache(maxsize=None)
def all_tables():
    w, deriv, basis, lam, hat = spectral_tables()
    denom = (
        STRETCH[0] * lam[:, None, None] + STRETCH[1] * lam[None, :, None] + STRETCH[2] * lam[None, None, :]
    )
    big = np.kron(np.kron(basis, basis), basis)
    full = ((big / denom.reshape(1, 512)) @ big.T).reshape(8, 8, 8, 8, 8, 8)
    local_solve = []
    for si in (1.0, -1.0):
        for sj in (1.0, -1.0):
            t = full[:4, :4]
            t = 0.5 * (t[:, :, :, :4] + si * t[:, :, :, 7:3:-1])
            t = 0.5 * (t[:, :, :, :, :4] + sj * t[:, :, :, :, 7:3:-1])
            local_solve.append(t.reshape(128, 128))
    local_solve = np.stack(local_solve)
    tx, sx, mx = sine_system(EX)
    ty, sy, my = sine_system(EY)
    tz, sz, mz = sine_system(EZ)
    vx = np.zeros((EX + 1, EX - 1))
    vx[1:-1] = tx
    vy = np.zeros((EY + 1, EY - 1))
    vy[1:-1] = ty
    vz = np.zeros((EZ + 1, EZ))
    vz[1:-1, : EZ - 1] = tz
    z_low, z_high = vz[:-1], vz[1:]
    eig = (
        STRETCH[0] * sx[:, None, None] * my[None, :, None] * mz[None, None, :]
        + STRETCH[1] * mx[:, None, None] * sy[None, :, None] * mz[None, None, :]
        + STRETCH[2] * mx[:, None, None] * my[None, :, None] * sz[None, None, :]
    )
    inv_eig = np.zeros((MODES_PAD, EZ))
    inv_eig[:MODES, : EZ - 1] = (1.0 / eig).reshape(MODES, EZ - 1)
    part = np.zeros((MODES, EX // 2, EY, 2, 2))
    for a in range(2):
        for b in range(2):
            rows_x = vx[a : a + EX - 1 : 2]
            rows_y = vy[b : b + EY]
            part[:, :, :, a, b] = np.einsum("xm,yn->mnxy", rows_x, rows_y).reshape(MODES, EX // 2, EY)
    gather = np.zeros((MODES_PAD, 4 * CHIPS))
    gather[:MODES] = part.reshape(MODES, 4 * CHIPS)
    flip = np.array([1.0 if m % 2 == 0 else -1.0 for m in range(EX - 1)])
    own_x = np.zeros((EX, 8, MODES_PAD))
    for x in range(EX):
        for row in range(8):
            side, a = row // 4, row // 2 % 2
            sign = flip if x % 2 else 1.0
            own_x[x, row, :MODES] = np.repeat(sign * vx[(x ^ side) + a], EY - 1)
    own_y = np.zeros((EY + 8, MODES_PAD))
    own_y[: EY + 1, :MODES] = np.tile(vy, (1, EX - 1))
    lanes = np.ones((1, 128))
    roll_tables = np.zeros((19, 8, 128))
    for s in range(8):
        for r in range(8):
            roll_tables[s, r] = deriv[r, (r - s) % 8]
            roll_tables[8 + s, r] = deriv[(r - s) % 8, r]
    roll_tables[16] = hat[0][:, None] * lanes
    roll_tables[17] = hat[1][:, None] * lanes
    roll_tables[18] = w[:, None] * lanes
    f = lambda t: np.asarray(t, np.float32)

    def split(t):
        high = t.astype(BF16)
        return np.stack([high, (t - high.astype(np.float64)).astype(BF16)])

    return dict(
        deriv=f(deriv),
        hat=f(hat),
        local_solve=split(local_solve),
        z_in=split(np.concatenate([z_low, z_high], axis=1)),
        z_out=split(np.concatenate([z_low.T, z_high.T], axis=1)),
        inv_eig=f(inv_eig),
        gather=split(gather),
        own_x=f(own_x),
        own_y=f(own_y),
        rolls=f(roll_tables),
        weight=w,
    )


FACE = jax.ShapeDtypeStruct((8, 8, 128), F32)
FACES = (FACE,) * 4
NODES = jax.ShapeDtypeStruct((8, 8, 8, 128), F32)
ROWS = jax.ShapeDtypeStruct((4 * CHIPS, 128), F32)
SMALL = jax.ShapeDtypeStruct((8, 128), F32)
VMEM = pl.BlockSpec(memory_space=pltpu.VMEM)
SMEM = pl.BlockSpec(memory_space=pltpu.SMEM)


def call(body, outs, place, *args, scratch=(), specs=None):
    return pl.pallas_call(
        body,
        out_shape=outs,
        in_specs=[SMEM] + (specs or [VMEM] * len(args)),
        out_specs=[VMEM] * len(outs),
        scratch_shapes=list(scratch),
        compiler_params=pltpu.CompilerParams(vmem_limit_bytes=12 << 20),
    )(place, *args)


def parts(x):
    high = x.astype(jnp.bfloat16)
    return high, (x - high.astype(F32)).astype(jnp.bfloat16)


def dot(a, b):
    return jnp.dot(a, b, preferred_element_type=F32)


def table_dot(table, x):
    high, low = parts(x)
    return dot(table[0], high) + (dot(table[0], low) + dot(table[1], high))


def dot_table(x, table):
    high, low = parts(x)
    first = dot(jnp.concatenate([high, low], axis=0), table[0])
    return first[0:8] + (first[8:16] + dot(high, table[1]))


def inner_x(place):
    return 7 * (1 - (place[0] & 1))


def inner_y(place):
    return 7 * (1 - (place[1] & 1))


def put_faces(place, u, faces):
    xin, xout, yin, yout = faces
    ax, ay = inner_x(place), inner_y(place)
    xin[...] = u[ax]
    xout[...] = u[7 - ax]
    for i in range(8):
        yin[i] = u[i, ay]
        yout[i] = u[i, 7 - ay]


def lane_iota():
    return lax.broadcasted_iota(jnp.int32, (8, 128), 1)


def row_iota():
    return lax.broadcasted_iota(jnp.int32, (8, 128), 0)


def weighted(coefs, vals):
    out = None
    for c, v in zip(coefs, vals):
        if c != 0.0:
            t = v if c == 1.0 else float(c) * v
            out = t if out is None else out + t
    return out


def restrict_rows(place, u, rolls, z_in):
    hat = all_tables()["hat"]
    near = [[weighted(hat[b], [u[i, j] for j in range(8)]) for i in range(8)] for b in range(2)]
    corner = [[weighted(hat[a], near[b]) for b in range(2)] for a in range(2)]
    row = row_iota()
    odd = (place[0] & 1) == 1
    out = jnp.zeros((8, 128), F32)
    for c in range(2):
        for a in range(2):
            for b in range(2):
                line = jnp.sum(rolls[16 + c] * corner[a][b], axis=0, keepdims=True)
                at = jnp.where(odd, 4 * c + 2 * (1 - a) + b, 4 * c + 2 * a + b)
                out = jnp.where(row == at, line, out)
    modes = dot_table(out, z_in)
    return modes[0:4, 0:128] + modes[4:8, 128:256]


def send_rows(rows, out):
    pair = jnp.concatenate([rows, rows], axis=0)
    for t in range(4 * CHIPS // 8):
        out[8 * t : 8 * t + 8] = pair


def assemble(place, u, xin, xout, yin, yout, v):
    ax, ay = inner_x(place), inner_y(place)
    keep_x = jnp.where((place[0] == 0) | (place[0] == EX - 1), 0.0, 1.0).astype(F32)
    keep_y = jnp.where((place[1] == 0) | (place[1] == EY - 1), 0.0, 1.0).astype(F32)
    v[...] = u[...]
    v[ax] = v[ax] + xin[...]
    v[7 - ax] = (v[7 - ax] + xout[...]) * keep_x
    for i in range(8):
        v[i, ay] = v[i, ay] + yin[i]
        v[i, 7 - ay] = (v[i, 7 - ay] + yout[i]) * keep_y
    v[7 - ax] = v[7 - ax] * keep_x
    lane, row = lane_iota(), row_iota()
    first, last = row == 0, row == 7
    keep_z = jnp.where((first & (lane == 0)) | (last & (lane == 127)), 0.0, 1.0).astype(F32)
    for i in range(8):
        for j in range(8):
            t = v[i, j]
            from_prev = pltpu.roll(pltpu.roll(t, 1, 1), 1, 0)
            from_next = pltpu.roll(pltpu.roll(t, 127, 1), 7, 0)
            t = t + jnp.where(first, from_prev, 0.0) + jnp.where(last, from_next, 0.0)
            v[i, j] = t * keep_z


def lines(vals, weights, deriv):
    even = 0.5 * (deriv[:4, :4] + deriv[:4, 7:3:-1])
    odd = 0.5 * (deriv[:4, :4] - deriv[:4, 7:3:-1])
    sums = [vals[i] + vals[7 - i] for i in range(4)]
    difs = [vals[i] - vals[7 - i] for i in range(4)]
    u, v = [], []
    for p in range(4):
        e, o = weighted(even[p], sums), weighted(odd[p], difs)
        q, r = (o + e) * weights[p], (o - e) * weights[7 - p]
        u.append(q - r)
        v.append(q + r)
    out = [None] * 8
    for i in range(4):
        e, o = weighted(even[:, i], u), weighted(odd[:, i], v)
        out[i], out[7 - i] = e + o, e - o
    return out


def stiffness(u, cw, rolls, out):
    deriv = all_tables()["deriv"].astype(np.float64)
    for j in range(8):
        r = lines([u[i, j] for i in range(8)], [cw[i, j] for i in range(8)], deriv)
        for i in range(8):
            out[i, j] = r[i]
    for i in range(8):
        r = lines([u[i, j] for j in range(8)], [cw[i, j] for j in range(8)], deriv)
        for j in range(8):
            t = u[i, j]
            g = rolls[0] * t
            for s in range(1, 8):
                g = g + rolls[s] * pltpu.roll(t, s, 0)
            q = g * cw[i, j]
            k = rolls[8] * q
            for s in range(1, 8):
                k = k + rolls[8 + s] * pltpu.roll(q, s, 0)
            out[i, j] = out[i, j] + (STRETCH[1] * r[j] + k)


def prolong_add(coarse, rolls, z_out, v):
    hat = all_tables()["hat"]
    both = dot_table(coarse, z_out)
    low, high = both[:, 0:128], both[:, 128:256]
    h0, h1 = rolls[16], rolls[17]
    line = [h0 * low[r : r + 1] + h1 * high[r : r + 1] for r in range(4)]
    for j in range(8):
        near = float(hat[0, j]) * line[0] + float(hat[1, j]) * line[1]
        far = float(hat[0, j]) * line[2] + float(hat[1, j]) * line[3]
        for i in range(8):
            v[i, j] = v[i, j] + (float(hat[0, i]) * near + float(hat[1, i]) * far)


def total(a, b):
    return jnp.sum(a[...] * b[...], keepdims=True).reshape(1, 1)


def k_faces(place, u, xin, xout, yin, yout, sems):
    ax, ay = inner_x(place), inner_y(place)
    sources = (u.at[ax], u.at[7 - ax], u.at[:, ay], u.at[:, 7 - ay])
    copies = [
        pltpu.make_async_copy(source, face, sems.at[n])
        for n, (source, face) in enumerate(zip(sources, (xin, xout, yin, yout)))
    ]
    for copy in copies:
        copy.start()
    for copy in copies:
        copy.wait()


def k_restrict(place, u, rolls, z_in, rows):
    send_rows(restrict_rows(place, u, rolls, z_in), rows)


def k_weight(place, coefficient, rolls, cw):
    w = all_tables()["weight"]
    for i in range(8):
        for j in range(8):
            cw[i, j] = coefficient[i, j] * (float(w[i] * w[j]) * rolls[18])


def k_local_solve(place, u, xin, xout, yin, yout, solve, v, h, *faces):
    assemble(place, u, xin, xout, yin, yout, v)
    out = []
    for si in range(2):
        for sj in range(2):
            block = []
            for i in range(4):
                for j in range(4):
                    near, far = v[i, j], v[7 - i, j]
                    near_j, far_j = v[i, 7 - j], v[7 - i, 7 - j]
                    left = near - far if si else near + far
                    right = near_j - far_j if si else near_j + far_j
                    block.append(left - right if sj else left + right)
            high, low = parts(jnp.concatenate(block, axis=0))
            t, t_low = solve[0, 2 * si + sj], solve[1, 2 * si + sj]
            out.append((dot(t, high) + (dot(t, low) + dot(t_low, high))).reshape(4, 4, 8, 128))
    for i in range(4):
        for j in range(4):
            pp, pm, mp, mm = (block[i, j] for block in out)
            a, b, c, d = pp + pm, pp - pm, mp + mm, mp - mm
            h[i, j] = a + c
            h[7 - i, j] = a - c
            h[i, 7 - j] = b + d
            h[7 - i, 7 - j] = b - d
    put_faces(place, h, faces)


def k_coarse(place, got, gather, inv_eig, own_x, own_y, out):
    core = place[2]
    size = CHIPS
    blocks = [got[pl.ds(pl.multiple_of(size * (n + core * (3 - 2 * n)), size), size)] for n in range(4)]
    modes = table_dot(gather, jnp.concatenate(blocks, axis=0)) * inv_eig[...]
    row = lax.broadcasted_iota(jnp.int32, (8, MODES_PAD), 0)
    low, high = own_y[pl.ds(place[1], 1)], own_y[pl.ds(place[1] + 1, 1)]
    own = own_x[place[0]] * jnp.where((row & 1) == 0, low, high)
    own_high, own_low = parts(own)
    high, low = parts(modes)
    first = dot(jnp.concatenate([own_high, own_low], axis=0), high)
    mine = first[0:8] + (first[8:16] + dot(own_high, low))
    sums = jnp.sum(got[...].reshape(4 * CHIPS // 8, 8, 128), axis=0)
    sums = sums + pltpu.roll(sums, 4, 0)
    out[...] = jnp.where(lane_iota() == 127, sums, mine)


def both_halves(mine, theirs):
    return mine[...] + pltpu.roll(theirs[...], 4, 0)


def k_first(
    place, h, xin, xout, yin, yout, mine, theirs, f, cw, rolls, z_out, z_in, s, g, rows, *faces
):
    assemble(place, h, xin, xout, yin, yout, s)
    prolong_add(both_halves(mine, theirs), rolls, z_out, s)
    stiffness(s, cw, rolls, g)
    put_faces(place, g, faces)
    modes = restrict_rows(place, g, rolls, z_in)
    lane, row = lax.broadcasted_iota(jnp.int32, (4, 128), 1), lax.broadcasted_iota(jnp.int32, (4, 128), 0)
    sums = jnp.where(row == 0, total(f, s), jnp.where(row == 1, total(s, g), 0.0))
    send_rows(jnp.where(lane == 127, sums, modes), rows)


def k_second(
    place, h, xin, xout, yin, yout, mine, theirs, f, s0, g0, cw, rolls, z_out,
    s1, h1, rows, scalars, *rest,
):
    faces, t = rest[:4], rest[4]
    assemble(place, h, xin, xout, yin, yout, t)
    coarse = both_halves(mine, theirs)
    prolong_add(coarse, rolls, z_out, t)
    lane = lane_iota()
    known = jnp.sum(jnp.where(lane == 127, coarse, 0.0), axis=1, keepdims=True)
    energy, curve = known[0:1], known[1:2]
    step = energy / curve
    s1[...] = s0[...] - step * t[...]
    stiffness(s1, cw, rolls, h1)
    put_faces(place, h1, faces)
    fresh = jnp.sum(s1[...] * (f[...] - step * g0[...]), keepdims=True).reshape(1, 1)
    sums = (fresh, total(s1, h1), total(s1, g0), total(s0, h1))
    row = jnp.zeros((8, 128), F32)
    for n, value in enumerate(sums):
        row = jnp.where(lane == n, value, row)
    for n in range(2 * CHIPS // 8):
        rows[8 * n : 8 * n + 8] = row
    scalars[...] = jnp.where(lane == 0, energy, jnp.where(lane == 1, curve, step))


def k_last(place, h, xin, xout, yin, yout, got, scalars, s0, s1, b, w, p, r):
    sums = jnp.sum(got[...], axis=0, keepdims=True)
    fresh, s1h1, s1g0, s0h1 = (sums[:, n : n + 1] for n in range(4))
    energy, curve, step0 = (scalars[0:1, n : n + 1] for n in range(3))
    beta = fresh / energy
    step1 = fresh / (s1h1 + beta * (s1g0 + s0h1) + beta * beta * curve)
    assemble(place, h, xin, xout, yin, yout, r)
    p[...] = step0 * s0[...] + step1 * (s1[...] + beta * s0[...])
    r[...] = (b[...] - step0 * w[...]) - step1 * (r[...] + beta * w[...])


CHIP_AXES = ("x", "y", "z")
ALL_AXES = ("x", "c", "y", "z")
SWAP = [(0, 1), (1, 0)]


def swaps(along_x, start):
    out = []
    for x in range(EX):
        for y in range(EY):
            n, count = (x, EX) if along_x else (y, EY)
            other = (n - start ^ 1) + start
            if 0 <= other < count:
                to = (other, y) if along_x else (x, other)
            else:
                to = (x, y ^ 1) if along_x else (x ^ 1, y)
            out.append((x * EY + y, to[0] * EY + to[1]))
    return out


def swap_x(inner, outer):
    far = lax.ppermute(outer, ALL_AXES, swaps(True, 1))
    near = lax.ppermute(inner, "c", SWAP)
    return near, far


def swap_y(inner, outer):
    far = lax.ppermute(outer, ALL_AXES, swaps(False, 1))
    near = lax.ppermute(inner, ALL_AXES, swaps(False, 0))
    return near, far


def share(rows):
    got = lax.all_to_all(rows.reshape(CHIPS, 4, 128), CHIP_AXES, 0, 0)
    return got.reshape(4 * CHIPS, 128)


def on_device(forcing, coefficient):
    tables = all_tables()
    tab = lambda *names: [jnp.asarray(tables[n]) for n in names]
    f = forcing.reshape(8, 8, 8, 128)
    coef = coefficient.reshape(8, 8, 8, 128)
    px = lax.axis_index(("x", "c")).astype(jnp.int32)
    py = lax.axis_index(("y", "z")).astype(jnp.int32)
    n = jnp.arange(4, dtype=jnp.int32)
    place = jnp.where(n == 0, px, jnp.where(n == 1, py, px & 1))

    inside = jnp.arange(8, dtype=jnp.int32)[:, None, None] == 7 * (1 - (px & 1))
    outside = jnp.arange(8, dtype=jnp.int32)[:, None, None] == 7 * (px & 1)
    even = (py & 1) == 0

    def y_face(raw, last, xin, xout):
        near = jnp.where(last, xin[7], xin[0])[None]
        far = jnp.where(last, xout[7], xout[0])[None]
        return raw + jnp.where(inside, near, jnp.where(outside, far, 0.0))

    def halo(xin, xout, yin, yout):
        xs = swap_x(xin, xout)
        ys = swap_y(y_face(yin, even, *xs), y_face(yout, ~even, *xs))
        return xs + ys

    def coarse(rows):
        got = share(rows)
        mine = call(k_coarse, (SMALL,), place, got, *tab("gather", "inv_eig", "own_x", "own_y"))[0]
        return mine, lax.ppermute(mine, "c", SWAP)

    def local(u, sides):
        out = call(k_local_solve, (NODES, NODES) + FACES, place, u, *sides, *tab("local_solve"))
        return out[0], out[1], out[2:]

    faces = call(
        k_faces, FACES, place, f,
        specs=[pl.BlockSpec(memory_space=pltpu.HBM)], scratch=(pltpu.SemaphoreType.DMA((4,)),),
    )
    f_later, xin = lax.optimization_barrier((f, faces[0]))
    faces = (xin, *faces[1:])
    rows = call(k_restrict, (ROWS,), place, f_later, *tab("rolls", "z_in"))[0]
    cw = call(k_weight, (NODES,), place, coef, *tab("rolls"))[0]
    c0 = coarse(rows)
    b, h, faces = local(f, halo(*faces))
    s0, g0, rows, *faces1 = call(
        k_first, (NODES, NODES, ROWS) + FACES, place, h, *halo(*faces), *c0, f, cw,
        *tab("rolls", "z_out", "z_in"),
    )
    c1 = coarse(rows)
    w, h, faces = local(g0, halo(*faces1))
    s1, h1, rows, scalars, *faces1 = call(
        k_second,
        (NODES, NODES, jax.ShapeDtypeStruct((2 * CHIPS, 128), F32), SMALL) + FACES,
        place, h, *halo(*faces), *c1, f, s0, g0, cw, *tab("rolls", "z_out"),
        scratch=(pltpu.VMEM((8, 8, 8, 128), F32),),
    )
    got = lax.all_to_all(rows.reshape(2 * CHIPS, 1, 128), ALL_AXES, 0, 0).reshape(2 * CHIPS, 128)
    sides = halo(*faces1)
    p, r = call(k_last, (NODES, NODES), place, h1, *sides, got, scalars, s0, s1, b, w)
    return p.reshape(forcing.shape), r.reshape(forcing.shape)


def solution(mesh):
    fine = Mesh(mesh.devices.reshape(4, 2, 4, 8), ALL_AXES)
    spec = P(None, None, None, ("x", "c"), ("y", "z"), None)
    return jax.shard_map(
        on_device, mesh=fine, in_specs=(spec, spec), out_specs=(spec, spec), check_vma=False
    )
```

```python
import functools
import math

import jax
import jax.numpy as jnp
import numpy as np
from jax import lax
from jax.experimental import pallas as pl
from jax.experimental.pallas import tpu as pltpu
from jax.sharding import Mesh
from jax.sharding import PartitionSpec as P


EX = 8
EY = 32
EZ = 128
STRETCH = (1.0, 64.0, 1.0)
CHIPS = 128
MODES = (EX - 1) * (EY - 1)
MODES_PAD = 224
F32 = jnp.float32
BF16 = jnp.bfloat16


def legendre(order, x):
    before, now = 1.0, x
    for n in range(2, order + 1):
        before, now = now, ((2 * n - 1) * x * now - (n - 1) * before) / n
    return now


def gll_points():
    points = [-1.0]
    for n in range(1, 7):
        x = -math.cos(math.pi * n / 7.0)
        for _ in range(60):
            x = x - (legendre(8, x) - legendre(6, x)) / (15.0 * legendre(7, x))
        points.append(x)
    points.append(1.0)
    return points


@functools.lru_cache(maxsize=None)
def spectral_tables():
    nodes = gll_points()
    values = [legendre(7, x) for x in nodes]
    w = np.array([2.0 / (56.0 * v * v) for v in values])
    deriv = np.zeros((8, 8))
    for i in range(8):
        for j in range(8):
            if i != j:
                deriv[i, j] = values[i] / (values[j] * (nodes[i] - nodes[j]))
    deriv[0, 0] = -14.0
    deriv[7, 7] = 14.0
    stiff = deriv.T @ np.diag(w) @ deriv
    stiff[0, 0] *= 2.0
    stiff[7, 7] *= 2.0
    root = 1.0 / np.sqrt(w)
    lam, vec = np.linalg.eigh(root[:, None] * stiff * root[None, :])
    basis = root[:, None] * vec
    x = np.array(nodes)
    hat = np.stack([(1.0 - x) / 2.0, (1.0 + x) / 2.0])
    hat[0, 7] = 0.0
    hat[1, 0] = 0.0
    return w, deriv, basis, lam, hat


def sine_system(cells):
    n = np.arange(1, cells)
    table = math.sqrt(2.0 / cells) * np.sin(math.pi * ((n[:, None] * n[None, :]) % (2 * cells)) / cells)
    cosines = np.cos(math.pi * n / cells)
    return table, (2.0 - 2.0 * cosines) / 2.0, 2.0 * (4.0 + 2.0 * cosines) / 6.0


@functools.lru_cache(maxsize=None)
def all_tables():
    w, deriv, basis, lam, hat = spectral_tables()
    denom = (
        STRETCH[0] * lam[:, None, None] + STRETCH[1] * lam[None, :, None] + STRETCH[2] * lam[None, None, :]
    )
    big = np.kron(np.kron(basis, basis), basis)
    full = ((big / denom.reshape(1, 512)) @ big.T).reshape(8, 8, 8, 8, 8, 8)
    local_solve = []
    for si in (1.0, -1.0):
        for sj in (1.0, -1.0):
            t = full[:4, :4]
            t = 0.5 * (t[:, :, :, :4] + si * t[:, :, :, 7:3:-1])
            t = 0.5 * (t[:, :, :, :, :4] + sj * t[:, :, :, :, 7:3:-1])
            local_solve.append(t.reshape(128, 128))
    local_solve = np.stack(local_solve)
    tx, sx, mx = sine_system(EX)
    ty, sy, my = sine_system(EY)
    tz, sz, mz = sine_system(EZ)
    vx = np.zeros((EX + 1, EX - 1))
    vx[1:-1] = tx
    vy = np.zeros((EY + 1, EY - 1))
    vy[1:-1] = ty
    vz = np.zeros((EZ + 1, EZ))
    vz[1:-1, : EZ - 1] = tz
    z_low, z_high = vz[:-1], vz[1:]
    eig = (
        STRETCH[0] * sx[:, None, None] * my[None, :, None] * mz[None, None, :]
        + STRETCH[1] * mx[:, None, None] * sy[None, :, None] * mz[None, None, :]
        + STRETCH[2] * mx[:, None, None] * my[None, :, None] * sz[None, None, :]
    )
    inv_eig = np.zeros((MODES_PAD, EZ))
    inv_eig[:MODES, : EZ - 1] = (1.0 / eig).reshape(MODES, EZ - 1)
    part = np.zeros((MODES, EX // 2, EY, 2, 2))
    for a in range(2):
        for b in range(2):
            rows_x = vx[a : a + EX - 1 : 2]
            rows_y = vy[b : b + EY]
            part[:, :, :, a, b] = np.einsum("xm,yn->mnxy", rows_x, rows_y).reshape(MODES, EX // 2, EY)
    gather = np.zeros((MODES_PAD, 4 * CHIPS))
    gather[:MODES] = part.reshape(MODES, 4 * CHIPS)
    flip = np.array([1.0 if m % 2 == 0 else -1.0 for m in range(EX - 1)])
    own_x = np.zeros((EX, 8, MODES_PAD))
    for x in range(EX):
        for row in range(8):
            side, a = row // 4, row // 2 % 2
            sign = flip if x % 2 else 1.0
            own_x[x, row, :MODES] = np.repeat(sign * vx[(x ^ side) + a], EY - 1)
    own_y = np.zeros((EY + 8, MODES_PAD))
    own_y[: EY + 1, :MODES] = np.tile(vy, (1, EX - 1))
    lanes = np.ones((1, 128))
    roll_tables = np.zeros((19, 8, 128))
    for s in range(8):
        for r in range(8):
            roll_tables[s, r] = deriv[r, (r - s) % 8]
            roll_tables[8 + s, r] = deriv[(r - s) % 8, r]
    roll_tables[16] = hat[0][:, None] * lanes
    roll_tables[17] = hat[1][:, None] * lanes
    roll_tables[18] = w[:, None] * lanes
    f = lambda t: np.asarray(t, np.float32)

    def split(t):
        high = t.astype(BF16)
        return np.stack([high, (t - high.astype(np.float64)).astype(BF16)])

    return dict(
        deriv=f(deriv),
        hat=f(hat),
        local_solve=split(local_solve),
        z_in=split(np.concatenate([z_low, z_high], axis=1)),
        z_out=split(np.concatenate([z_low.T, z_high.T], axis=1)),
        inv_eig=f(inv_eig),
        gather=split(gather),
        own_x=f(own_x),
        own_y=f(own_y),
        rolls=f(roll_tables),
        weight=w,
    )


FACE = jax.ShapeDtypeStruct((8, 8, 128), F32)
FACES = (FACE,) * 4
NODES = jax.ShapeDtypeStruct((8, 8, 8, 128), F32)
ROWS = jax.ShapeDtypeStruct((4 * CHIPS, 128), F32)
SMALL = jax.ShapeDtypeStruct((8, 128), F32)
VMEM = pl.BlockSpec(memory_space=pltpu.VMEM)


def where_am_i():
    x = lax.axis_index("x") * 2 + lax.axis_index("c")
    y = lax.axis_index("y") * 8 + lax.axis_index("z")
    return x.astype(jnp.int32), y.astype(jnp.int32), (x & 1).astype(jnp.int32)


def call(body, outs, *args, scratch=(), specs=None):
    def placed(*refs):
        body(where_am_i(), *refs)

    return pl.pallas_call(
        placed,
        out_shape=outs,
        in_specs=specs or [VMEM] * len(args),
        out_specs=[VMEM] * len(outs),
        scratch_shapes=list(scratch),
        compiler_params=pltpu.CompilerParams(vmem_limit_bytes=12 << 20),
    )(*args)


def parts(x):
    high = x.astype(jnp.bfloat16)
    return high, (x - high.astype(F32)).astype(jnp.bfloat16)


def dot(a, b):
    return jnp.dot(a, b, preferred_element_type=F32)


def table_dot(table, x):
    high, low = parts(x)
    return dot(table[0], high) + (dot(table[0], low) + dot(table[1], high))


def dot_table(x, table):
    high, low = parts(x)
    first = dot(jnp.concatenate([high, low], axis=0), table[0])
    return first[0:8] + (first[8:16] + dot(high, table[1]))


def inner_x(place):
    return 7 * (1 - (place[0] & 1))


def inner_y(place):
    return 7 * (1 - (place[1] & 1))


def put_faces(place, u, faces):
    xin, xout, yin, yout = faces
    ax, ay = inner_x(place), inner_y(place)
    xin[...] = u[ax]
    xout[...] = u[7 - ax]
    for i in range(8):
        yin[i] = u[i, ay]
        yout[i] = u[i, 7 - ay]


def lane_iota():
    return lax.broadcasted_iota(jnp.int32, (8, 128), 1)


def row_iota():
    return lax.broadcasted_iota(jnp.int32, (8, 128), 0)


def weighted(coefs, vals):
    out = None
    for c, v in zip(coefs, vals):
        if c != 0.0:
            t = v if c == 1.0 else float(c) * v
            out = t if out is None else out + t
    return out


def restrict_rows(place, u, rolls, z_in):
    hat = all_tables()["hat"]
    near = [[weighted(hat[b], [u[i, j] for j in range(8)]) for i in range(8)] for b in range(2)]
    corner = [[weighted(hat[a], near[b]) for b in range(2)] for a in range(2)]
    row = row_iota()
    odd = (place[0] & 1) == 1
    out = jnp.zeros((8, 128), F32)
    for c in range(2):
        for a in range(2):
            for b in range(2):
                line = jnp.sum(rolls[16 + c] * corner[a][b], axis=0, keepdims=True)
                at = jnp.where(odd, 4 * c + 2 * (1 - a) + b, 4 * c + 2 * a + b)
                out = jnp.where(row == at, line, out)
    modes = dot_table(out, z_in)
    return modes[0:4, 0:128] + modes[4:8, 128:256]


def send_rows(rows, out):
    pair = jnp.concatenate([rows, rows], axis=0)
    for t in range(4 * CHIPS // 8):
        out[8 * t : 8 * t + 8] = pair


def assemble(place, u, xin, xout, yin, yout, v):
    ax, ay = inner_x(place), inner_y(place)
    keep_x = jnp.where((place[0] == 0) | (place[0] == EX - 1), 0.0, 1.0).astype(F32)
    keep_y = jnp.where((place[1] == 0) | (place[1] == EY - 1), 0.0, 1.0).astype(F32)
    v[...] = u[...]
    v[ax] = v[ax] + xin[...]
    v[7 - ax] = (v[7 - ax] + xout[...]) * keep_x
    for i in range(8):
        v[i, ay] = v[i, ay] + yin[i]
        v[i, 7 - ay] = (v[i, 7 - ay] + yout[i]) * keep_y
    v[7 - ax] = v[7 - ax] * keep_x
    lane, row = lane_iota(), row_iota()
    first, last = row == 0, row == 7
    keep_z = jnp.where((first & (lane == 0)) | (last & (lane == 127)), 0.0, 1.0).astype(F32)
    for i in range(8):
        for j in range(8):
            t = v[i, j]
            from_prev = pltpu.roll(pltpu.roll(t, 1, 1), 1, 0)
            from_next = pltpu.roll(pltpu.roll(t, 127, 1), 7, 0)
            t = t + jnp.where(first, from_prev, 0.0) + jnp.where(last, from_next, 0.0)
            v[i, j] = t * keep_z


def lines(vals, weights, deriv):
    even = 0.5 * (deriv[:4, :4] + deriv[:4, 7:3:-1])
    odd = 0.5 * (deriv[:4, :4] - deriv[:4, 7:3:-1])
    sums = [vals[i] + vals[7 - i] for i in range(4)]
    difs = [vals[i] - vals[7 - i] for i in range(4)]
    u, v = [], []
    for p in range(4):
        e, o = weighted(even[p], sums), weighted(odd[p], difs)
        q, r = (o + e) * weights[p], (o - e) * weights[7 - p]
        u.append(q - r)
        v.append(q + r)
    out = [None] * 8
    for i in range(4):
        e, o = weighted(even[:, i], u), weighted(odd[:, i], v)
        out[i], out[7 - i] = e + o, e - o
    return out


def stiffness(u, cw, rolls, out):
    deriv = all_tables()["deriv"].astype(np.float64)
    for j in range(8):
        r = lines([u[i, j] for i in range(8)], [cw[i, j] for i in range(8)], deriv)
        for i in range(8):
            out[i, j] = r[i]
    for i in range(8):
        r = lines([u[i, j] for j in range(8)], [cw[i, j] for j in range(8)], deriv)
        for j in range(8):
            t = u[i, j]
            g = rolls[0] * t
            for s in range(1, 8):
                g = g + rolls[s] * pltpu.roll(t, s, 0)
            q = g * cw[i, j]
            k = rolls[8] * q
            for s in range(1, 8):
                k = k + rolls[8 + s] * pltpu.roll(q, s, 0)
            out[i, j] = out[i, j] + (STRETCH[1] * r[j] + k)


def prolong_add(coarse, rolls, z_out, v):
    hat = all_tables()["hat"]
    both = dot_table(coarse, z_out)
    low, high = both[:, 0:128], both[:, 128:256]
    h0, h1 = rolls[16], rolls[17]
    line = [h0 * low[r : r + 1] + h1 * high[r : r + 1] for r in range(4)]
    for j in range(8):
        near = float(hat[0, j]) * line[0] + float(hat[1, j]) * line[1]
        far = float(hat[0, j]) * line[2] + float(hat[1, j]) * line[3]
        for i in range(8):
            v[i, j] = v[i, j] + (float(hat[0, i]) * near + float(hat[1, i]) * far)


def total(a, b):
    return jnp.sum(a[...] * b[...], keepdims=True).reshape(1, 1)


def k_faces(place, u, xin, xout, yin, yout, sems):
    ax, ay = inner_x(place), inner_y(place)
    sources = (u.at[ax], u.at[7 - ax], u.at[:, ay], u.at[:, 7 - ay])
    copies = [
        pltpu.make_async_copy(source, face, sems.at[n])
        for n, (source, face) in enumerate(zip(sources, (xin, xout, yin, yout)))
    ]
    for copy in copies:
        copy.start()
    for copy in copies:
        copy.wait()


def k_restrict(place, u, rolls, z_in, rows):
    send_rows(restrict_rows(place, u, rolls, z_in), rows)


def k_weight(place, coefficient, rolls, cw):
    w = all_tables()["weight"]
    for i in range(8):
        for j in range(8):
            cw[i, j] = coefficient[i, j] * (float(w[i] * w[j]) * rolls[18])


def k_local_solve(place, u, xin, xout, yin, yout, solve, v, h, *faces):
    assemble(place, u, xin, xout, yin, yout, v)
    out = []
    for si in range(2):
        for sj in range(2):
            block = []
            for i in range(4):
                for j in range(4):
                    near, far = v[i, j], v[7 - i, j]
                    near_j, far_j = v[i, 7 - j], v[7 - i, 7 - j]
                    left = near - far if si else near + far
                    right = near_j - far_j if si else near_j + far_j
                    block.append(left - right if sj else left + right)
            high, low = parts(jnp.concatenate(block, axis=0))
            t, t_low = solve[0, 2 * si + sj], solve[1, 2 * si + sj]
            out.append((dot(t, high) + (dot(t, low) + dot(t_low, high))).reshape(4, 4, 8, 128))
    for i in range(4):
        for j in range(4):
            pp, pm, mp, mm = (block[i, j] for block in out)
            a, b, c, d = pp + pm, pp - pm, mp + mm, mp - mm
            h[i, j] = a + c
            h[7 - i, j] = a - c
            h[i, 7 - j] = b + d
            h[7 - i, 7 - j] = b - d
    put_faces(place, h, faces)


def k_coarse(place, got, gather, inv_eig, own_x, own_y, out):
    core = place[2]
    size = CHIPS
    blocks = [got[pl.ds(pl.multiple_of(size * (n + core * (3 - 2 * n)), size), size)] for n in range(4)]
    modes = table_dot(gather, jnp.concatenate(blocks, axis=0)) * inv_eig[...]
    row = lax.broadcasted_iota(jnp.int32, (8, MODES_PAD), 0)
    low, high = own_y[pl.ds(place[1], 1)], own_y[pl.ds(place[1] + 1, 1)]
    own = own_x[place[0]] * jnp.where((row & 1) == 0, low, high)
    own_high, own_low = parts(own)
    high, low = parts(modes)
    first = dot(jnp.concatenate([own_high, own_low], axis=0), high)
    mine = first[0:8] + (first[8:16] + dot(own_high, low))
    sums = jnp.sum(got[...].reshape(4 * CHIPS // 8, 8, 128), axis=0)
    sums = sums + pltpu.roll(sums, 4, 0)
    out[...] = jnp.where(lane_iota() == 127, sums, mine)


def both_halves(mine, theirs):
    return mine[...] + pltpu.roll(theirs[...], 4, 0)


def k_first(
    place, h, xin, xout, yin, yout, mine, theirs, f, cw, rolls, z_out, z_in, s, g, rows, *faces
):
    assemble(place, h, xin, xout, yin, yout, s)
    prolong_add(both_halves(mine, theirs), rolls, z_out, s)
    stiffness(s, cw, rolls, g)
    put_faces(place, g, faces)
    modes = restrict_rows(place, g, rolls, z_in)
    lane, row = lax.broadcasted_iota(jnp.int32, (4, 128), 1), lax.broadcasted_iota(jnp.int32, (4, 128), 0)
    sums = jnp.where(row == 0, total(f, s), jnp.where(row == 1, total(s, g), 0.0))
    send_rows(jnp.where(lane == 127, sums, modes), rows)


def k_second(
    place, h, xin, xout, yin, yout, mine, theirs, f, s0, g0, cw, rolls, z_out,
    s1, h1, rows, scalars, *rest,
):
    faces, t = rest[:4], rest[4]
    assemble(place, h, xin, xout, yin, yout, t)
    coarse = both_halves(mine, theirs)
    prolong_add(coarse, rolls, z_out, t)
    lane = lane_iota()
    known = jnp.sum(jnp.where(lane == 127, coarse, 0.0), axis=1, keepdims=True)
    energy, curve = known[0:1], known[1:2]
    step = energy / curve
    s1[...] = s0[...] - step * t[...]
    stiffness(s1, cw, rolls, h1)
    put_faces(place, h1, faces)
    fresh = jnp.sum(s1[...] * (f[...] - step * g0[...]), keepdims=True).reshape(1, 1)
    sums = (fresh, total(s1, h1), total(s1, g0), total(s0, h1))
    row = jnp.zeros((8, 128), F32)
    for n, value in enumerate(sums):
        row = jnp.where(lane == n, value, row)
    for n in range(2 * CHIPS // 8):
        rows[8 * n : 8 * n + 8] = row
    scalars[...] = jnp.where(lane == 0, energy, jnp.where(lane == 1, curve, step))


def k_last(place, h, xin, xout, yin, yout, got, scalars, s0, s1, b, w, p, r):
    sums = jnp.sum(got[...], axis=0, keepdims=True)
    fresh, s1h1, s1g0, s0h1 = (sums[:, n : n + 1] for n in range(4))
    energy, curve, step0 = (scalars[0:1, n : n + 1] for n in range(3))
    beta = fresh / energy
    step1 = fresh / (s1h1 + beta * (s1g0 + s0h1) + beta * beta * curve)
    assemble(place, h, xin, xout, yin, yout, r)
    p[...] = step0 * s0[...] + step1 * (s1[...] + beta * s0[...])
    r[...] = (b[...] - step0 * w[...]) - step1 * (r[...] + beta * w[...])


CHIP_AXES = ("x", "y", "z")
ALL_AXES = ("x", "c", "y", "z")
SWAP = [(0, 1), (1, 0)]


def swaps(along_x, start):
    out = []
    for x in range(EX):
        for y in range(EY):
            n, count = (x, EX) if along_x else (y, EY)
            other = (n - start ^ 1) + start
            if 0 <= other < count:
                to = (other, y) if along_x else (x, other)
            else:
                to = (x, y ^ 1) if along_x else (x ^ 1, y)
            out.append((x * EY + y, to[0] * EY + to[1]))
    return out


def swap_x(inner, outer):
    far = lax.ppermute(outer, ALL_AXES, swaps(True, 1))
    near = lax.ppermute(inner, "c", SWAP)
    return near, far


def swap_y(inner, outer):
    far = lax.ppermute(outer, ALL_AXES, swaps(False, 1))
    near = lax.ppermute(inner, ALL_AXES, swaps(False, 0))
    return near, far


def share(rows):
    got = lax.all_to_all(rows.reshape(CHIPS, 4, 128), CHIP_AXES, 0, 0)
    return got.reshape(4 * CHIPS, 128)


def on_device(forcing, coefficient):
    tables = all_tables()
    tab = lambda *names: [jnp.asarray(tables[n]) for n in names]
    f = forcing.reshape(8, 8, 8, 128)
    coef = coefficient.reshape(8, 8, 8, 128)
    px, py, _ = where_am_i()
    inside = jnp.arange(8, dtype=jnp.int32)[:, None, None] == 7 * (1 - (px & 1))
    outside = jnp.arange(8, dtype=jnp.int32)[:, None, None] == 7 * (px & 1)
    even = (py & 1) == 0

    def y_face(raw, last, xin, xout):
        near = jnp.where(last, xin[7], xin[0])[None]
        far = jnp.where(last, xout[7], xout[0])[None]
        return raw + jnp.where(inside, near, jnp.where(outside, far, 0.0))

    def halo(xin, xout, yin, yout):
        xs = swap_x(xin, xout)
        ys = swap_y(y_face(yin, even, *xs), y_face(yout, ~even, *xs))
        return xs + ys

    def coarse(rows):
        got = share(rows)
        mine = call(k_coarse, (SMALL,), got, *tab("gather", "inv_eig", "own_x", "own_y"))[0]
        return mine, lax.ppermute(mine, "c", SWAP)

    def local(u, sides):
        out = call(k_local_solve, (NODES, NODES) + FACES, u, *sides, *tab("local_solve"))
        return out[0], out[1], out[2:]

    faces = call(
        k_faces, FACES, f,
        specs=[pl.BlockSpec(memory_space=pltpu.HBM)], scratch=(pltpu.SemaphoreType.DMA((4,)),),
    )
    f_later, xin = lax.optimization_barrier((f, faces[0]))
    faces = (xin, *faces[1:])
    rows = call(k_restrict, (ROWS,), f_later, *tab("rolls", "z_in"))[0]
    cw = call(k_weight, (NODES,), coef, *tab("rolls"))[0]
    c0 = coarse(rows)
    b, h, faces = local(f, halo(*faces))
    s0, g0, rows, *faces1 = call(
        k_first, (NODES, NODES, ROWS) + FACES, h, *halo(*faces), *c0, f, cw,
        *tab("rolls", "z_out", "z_in"),
    )
    c1 = coarse(rows)
    w, h, faces = local(g0, halo(*faces1))
    s1, h1, rows, scalars, *faces1 = call(
        k_second,
        (NODES, NODES, jax.ShapeDtypeStruct((2 * CHIPS, 128), F32), SMALL) + FACES,
        h, *halo(*faces), *c1, f, s0, g0, cw, *tab("rolls", "z_out"),
        scratch=(pltpu.VMEM((8, 8, 8, 128), F32),),
    )
    got = lax.all_to_all(rows.reshape(2 * CHIPS, 1, 128), ALL_AXES, 0, 0).reshape(2 * CHIPS, 128)
    sides = halo(*faces1)
    p, r = call(k_last, (NODES, NODES), h1, *sides, got, scalars, s0, s1, b, w)
    return p.reshape(forcing.shape), r.reshape(forcing.shape)


def solution(mesh):
    fine = Mesh(mesh.devices.reshape(4, 2, 4, 8), ALL_AXES)
    spec = P(None, None, None, ("x", "c"), ("y", "z"), None)
    return jax.shard_map(
        on_device, mesh=fine, in_specs=(spec, spec), out_specs=(spec, spec), check_vma=False
    )
```
